32 devices in a mesh: depth: 8 (over y, x, core), kslab: 4 (over z).
Axes of the slice: x: 2, y: 2, z: 4, core: 2. Of those that a mesh axis runs over, the one named last changes fastest.
Arguments:
- spectra: bfloat16 [8, 2, 512, 1024], P('depth', None, 'kslab'), may hold values from -6 to 6
- green: bfloat16 [8, 8, 2, 512, 1024], P('depth', None, None, 'kslab'), may hold values from -1 to 1, as said below
- contrast: float32 [8, 512, 1024], P('depth', None, 'kslab'), may hold values from 0.3 to 3
Outputs:
- applied: bfloat16 [8, 2, 512, 1024], P('depth', None, None, 'kslab')
The draws below stay inside these ranges and needn't reach their ends.
Inputs may be any that keep to these rules, and one draw needn't show every extreme that they name: green[t, s] equals green[s, t] for every pair of layers (reciprocity).
All inputs are finite; a program needn't handle non-finite values.
Results may differ from the reference program's by a relative error of at most 0.007.
Values may be sent and summed in bfloat16 or wider, within the bound.
No kernel may reach another device: no remote copies, remote signals or barrier semaphores. Data moves between devices by JAX's collectives and lax.ppermute only.
A program may use at most 128 MiB of HBM per device.

```python
import math
import jax
import jax.numpy as jnp
from jax import lax

NX = 512
NY = 1024
LAYERS = 8


def draw_green(key, part):
    layer_ids = jnp.arange(LAYERS, dtype=jnp.int32)

    def one_pair(target, source):
        lower_layer = jnp.minimum(target, source)
        upper_layer = jnp.maximum(target, source)
        pair_key = jax.random.fold_in(key, lower_layer * LAYERS + upper_layer)
        entries = jax.random.normal(pair_key, (2, NX, NY), jnp.float32)
        return jnp.clip(entries / math.sqrt(LAYERS), -1.0, 1.0).astype(jnp.bfloat16)

    def one_row(target):
        return jax.vmap(lambda source: one_pair(target, source))(layer_ids)
    return lax.map(one_row, layer_ids)


def level_of(key, dims, cuts, low, largest):
    loudness = 1.0
    for axis_at, parts in cuts:
        steps = jax.random.uniform(jax.random.fold_in(jax.random.fold_in(key, 6), axis_at), (parts,), jnp.float32, low / len(cuts), largest / len(cuts))
        loudness = loudness * jnp.repeat(jnp.exp(steps), dims[axis_at] // parts).reshape((-1,) + (1,) * (len(dims) - 1 - axis_at))
    return loudness


def bell_draw(rng, shape, spread, most, pieces=(), kind=jnp.bfloat16):
    result = jax.random.normal(rng, shape, jnp.float32) * spread
    if len(pieces) > 0:
        result = level_of(rng, shape, pieces, -0.22, 0.18) * result
    return jnp.clip(result, min=-most, max=most).astype(kind)


def setup_inputs(seed: int = 0) -> dict:
    keys = jax.random.split(jax.random.key(seed), 4)
    return {
        "spectra": bell_draw(keys[0], (LAYERS, 2, NX, NY), 1.0, 6.0, ((0, 8), (2, 4))),
        "green": draw_green(jax.random.fold_in(keys[3], 71), 0),
        "contrast": jnp.clip(jnp.exp(math.log(3.0) - 2.3025851 * jax.random.uniform(keys[2], (LAYERS, NX, NY), jnp.float32) ** level_of(keys[2], (LAYERS, NX, NY), ((0, 8), (2, 4)), -0.2, 0.2)), 0.3, 3.0),
    }


def fourier_tables(length):
    indices = jnp.arange(length, dtype=jnp.int32)
    products = indices[:, None] * indices[None, :] % length
    angles = products.astype(jnp.float32) * (2.0 * math.pi / length)
    factor = 1.0 / math.sqrt(length)
    return ((jnp.cos(angles) * factor).astype(jnp.bfloat16), (jnp.sin(angles) * factor).astype(jnp.bfloat16))

def reference(spectra, green, contrast):
    cos_y, sin_y = fourier_tables(NY)
    table_y = jnp.concatenate([cos_y, sin_y], axis=1)
    cos_x, sin_x = fourier_tables(NX)
    table_x = jnp.concatenate([cos_x, sin_x], axis=0)
    sources = spectra.astype(jnp.float32)

    def one_target(target):
        coeffs = green[target].astype(jnp.float32)
        real_part = lax.optimization_barrier(jnp.sum(coeffs[:, 0] * sources[:, 0] - coeffs[:, 1] * sources[:, 1], axis=0))
        imag_part = lax.optimization_barrier(jnp.sum(coeffs[:, 0] * sources[:, 1] + coeffs[:, 1] * sources[:, 0], axis=0))
        summed = jnp.stack([real_part, imag_part]).astype(jnp.bfloat16)
        section_one = jnp.dot(summed.reshape(2 * NX, NY), table_y, preferred_element_type=jnp.float32)
        halfway = jnp.stack([section_one[:NX, :NY] - section_one[NX:, NY:], section_one[:NX, NY:] + section_one[NX:, :NY]]).astype(jnp.bfloat16)
        from_real = jnp.dot(table_x, halfway[0], preferred_element_type=jnp.float32)
        from_imag = jnp.dot(table_x, halfway[1], preferred_element_type=jnp.float32)
        field_out = jnp.stack([from_real[:NX] - from_imag[NX:], from_real[NX:] + from_imag[:NX]])
        return (field_out * contrast[target][None]).astype(jnp.bfloat16)
    return lax.map(one_target, jnp.arange(LAYERS, dtype=jnp.int32))
```

```python
import math

import jax
import jax.numpy as jnp
from jax import lax
from jax.experimental import pallas as pl
from jax.experimental.pallas import tpu as pltpu
from jax.sharding import PartitionSpec as P


F32 = jnp.float32
BF16 = jnp.bfloat16
ROWS = 16
FINE = 32
MIB = 1 << 20


def fourier_tables(length):
    indices = jnp.arange(length, dtype=jnp.int32)
    products = indices[:, None] * indices[None, :] % length
    angles = products.astype(F32) * (2.0 * math.pi / length)
    factor = 1.0 / math.sqrt(length)
    return (jnp.cos(angles) * factor).astype(BF16), (jnp.sin(angles) * factor).astype(BF16)


def on_any_device(spectra, green, contrast):
    lay_dev, _, kx_dev, ny = spectra.shape
    nx = contrast.shape[1]
    coeffs = green.astype(F32)
    sources = lax.all_gather(spectra, "depth", axis=0, tiled=True).astype(F32)[None]
    real_part = jnp.sum(coeffs[:, :, 0] * sources[:, :, 0] - coeffs[:, :, 1] * sources[:, :, 1], axis=1)
    imag_part = jnp.sum(coeffs[:, :, 0] * sources[:, :, 1] + coeffs[:, :, 1] * sources[:, :, 0], axis=1)
    rounded = jnp.stack([real_part, imag_part], axis=1).astype(BF16)
    table_y = jnp.concatenate(fourier_tables(ny), axis=1)
    rows = lay_dev * kx_dev
    from_real = jnp.dot(rounded[:, 0].reshape(rows, ny), table_y, preferred_element_type=F32)
    from_imag = jnp.dot(rounded[:, 1].reshape(rows, ny), table_y, preferred_element_type=F32)
    halfway_real = (from_real[:, :ny] - from_imag[:, ny:]).reshape(lay_dev, kx_dev, ny)
    halfway_imag = (from_real[:, ny:] + from_imag[:, :ny]).reshape(lay_dev, kx_dev, ny)
    halfway = jnp.stack([halfway_real, halfway_imag], axis=1).astype(BF16)
    table_x = jnp.concatenate(fourier_tables(nx), axis=0)
    stacked = jnp.einsum(
        "ak,nckd->ncad",
        table_x,
        lax.all_to_all(halfway, "kslab", split_axis=3, concat_axis=2, tiled=True),
        preferred_element_type=F32,
    )
    real_part = stacked[:, 0, :nx] - stacked[:, 1, nx:]
    imag_part = stacked[:, 0, nx:] + stacked[:, 1, :nx]
    return (jnp.stack([real_part, imag_part], axis=1) * contrast[:, None]).astype(BF16)


def in_vmem(x):
    return pltpu.with_memory_space_constraint(x, pltpu.VMEM)


def call(body, outs, ins, scratch=(), flops=0, name=None, vmem=24 * MIB):
    spec = pl.BlockSpec(memory_space=pltpu.VMEM)
    moved = sum(math.prod(v.shape) * v.dtype.itemsize for v in list(outs) + list(ins))
    return pl.pallas_call(
        body,
        out_shape=[pltpu.VMEM(o.shape, o.dtype) for o in outs],
        in_specs=[spec] * len(ins),
        out_specs=[spec] * len(outs),
        scratch_shapes=list(scratch),
        compiler_params=pltpu.CompilerParams(vmem_limit_bytes=vmem),
        cost_estimate=pl.CostEstimate(flops=flops, bytes_accessed=moved, transcendentals=0),
        name=name,
    )(*[in_vmem(v) for v in ins])


def struct(shape, dtype):
    return jax.ShapeDtypeStruct(shape, dtype)


def modulo(v, length):
    return v & (length - 1) if length & (length - 1) == 0 else lax.rem(v, length)


def fill_table(length, columns, coarse_ref, put):
    width = columns.shape[1]
    step = 2.0 * math.pi / length
    factor = 1.0 / math.sqrt(length)
    rows = lax.broadcasted_iota(jnp.int32, (length // FINE, width), 0) * FINE
    angle = modulo(rows * columns, length).astype(F32) * step
    coarse_ref[0, pl.ds(0, length // FINE)] = jnp.cos(angle) * factor
    coarse_ref[1, pl.ds(0, length // FINE)] = jnp.sin(angle) * factor
    rows = lax.broadcasted_iota(jnp.int32, (FINE, width), 0)
    angle = modulo(rows * columns, length).astype(F32) * step
    coarse_ref[2, pl.ds(0, FINE)] = jnp.cos(angle)
    coarse_ref[3, pl.ds(0, FINE)] = jnp.sin(angle)

    @pl.loop(0, length // FINE)
    def _(block):
        for left in range(0, width, 256):
            cols = pl.ds(left, min(256, width - left))
            cos_c, sin_c = coarse_ref[0, pl.ds(block, 1), cols], coarse_ref[1, pl.ds(block, 1), cols]
            cos_f, sin_f = coarse_ref[2, pl.ds(0, FINE), cols], coarse_ref[3, pl.ds(0, FINE), cols]
            row = pl.ds(pl.multiple_of(block * FINE, FINE), FINE)
            put(row, left, cols, cos_c * cos_f - sin_c * sin_f, sin_c * cos_f + cos_c * sin_f)


def tables(nx, ny, kx_dev, parts, slabs):
    def body(ty_ref, *rest):
        tx_refs, (coarse_y, coarse_x) = rest[:-2], rest[-2:]
        z = lax.axis_index("kslab")
        wide = ny // slabs
        lane = lax.broadcasted_iota(jnp.int32, (1, ny), 1)
        columns = jnp.bitwise_xor(lane // wide, z) * wide + lane % wide

        def put_y(row, left, cols, cos, sin):
            ty_ref[0, row, cols] = cos.astype(BF16)
            ty_ref[1, row, cols] = sin.astype(BF16)

        fill_table(ny, columns, coarse_y, put_y)
        for (start, size), tx_ref in zip(parts, tx_refs):
            lane = lax.broadcasted_iota(jnp.int32, (1, slabs * size), 1)
            columns = jnp.bitwise_xor(lane // size, z) * kx_dev + start + lane % size

            def put_x(row, left, cols, cos, sin):
                tx_ref[0, row, cols] = cos.astype(BF16)
                tx_ref[1, row, cols] = sin.astype(BF16)

            fill_table(nx, columns, coarse_x.at[:, :, pl.ds(0, slabs * size)], put_x)

    outs = [struct((2, ny, ny), BF16)]
    outs += [struct((2, nx, slabs * size), BF16) for _, size in parts]
    most = max(size for _, size in parts)
    scratch = [
        pltpu.VMEM((4, max(ny // FINE, FINE), ny), F32),
        pltpu.VMEM((4, max(nx // FINE, FINE), slabs * most), F32),
    ]
    return call(body, outs, [], scratch, flops=8 * ny * ny, name="tables")


def add_sources(total, green_ref, sources, row, green_row, cols):
    real, imag = total
    for ref, layer in sources:
        g_real, g_imag = green_ref[layer, 0, green_row, cols].astype(F32), green_ref[layer, 1, green_row, cols].astype(F32)
        s_real, s_imag = ref[0, row, cols].astype(F32), ref[1, row, cols].astype(F32)
        p_real = g_real * s_real - g_imag * s_imag
        p_imag = g_real * s_imag + g_imag * s_real
        real = p_real if real is None else real + p_real
        imag = p_imag if imag is None else imag + p_imag
    return real, imag


def first_sum(green, arrays, layers):
    _, rows, ny = arrays[0].shape

    def body(green_ref, *refs):
        total_ref = refs[-1]
        sources = list(zip(refs[:-1], layers()))

        @pl.loop(0, rows // ROWS)
        def _(step):
            row = pl.ds(pl.multiple_of(step * ROWS, ROWS), ROWS)
            for left in range(0, ny, 256):
                cols = pl.ds(left, 256)
                total_ref[0, row, cols], total_ref[1, row, cols] = add_sources(
                    (None, None), green_ref, sources, row, row, cols
                )

    return call(body, [struct((2, rows, ny), F32)], [green, *arrays], flops=8 * len(arrays) * rows * ny, name="first_sum")[0]


def finish_rows(green, total, arrays, layers, table_y, start, slabs):
    _, size, ny = arrays[0].shape
    wide = ny // slabs

    def body(green_ref, total_ref, table_ref, *refs):
        ins, outs, left_ref = refs[: len(arrays)], refs[len(arrays) : -1], refs[-1]
        sources = list(zip(ins, layers()))

        @pl.loop(0, size // ROWS)
        def _(step):
            row = pl.ds(pl.multiple_of(step * ROWS, ROWS), ROWS)
            low = pl.ds(pl.multiple_of(size + step * ROWS, ROWS), ROWS)
            whole = pl.ds(pl.multiple_of(start + step * ROWS, ROWS), ROWS)
            for left in range(0, ny, 256):
                cols = pl.ds(left, 256)
                begun = total_ref[0, whole, cols], total_ref[1, whole, cols]
                real, imag = add_sources(begun, green_ref, sources, row, whole, cols)
                left_ref[row, pl.ds(left, 256)] = real.astype(BF16)
                left_ref[row, pl.ds(ny + left, 256)] = (-imag).astype(BF16)
                left_ref[low, pl.ds(left, 256)] = imag.astype(BF16)
                left_ref[low, pl.ds(ny + left, 256)] = real.astype(BF16)

        for m, out_ref in enumerate(outs):
            cols = pl.ds(m * wide, wide)
            both = jnp.dot(left_ref[:, pl.ds(0, ny)], table_ref[0, :, cols], preferred_element_type=F32)
            both += jnp.dot(left_ref[:, pl.ds(ny, ny)], table_ref[1, :, cols], preferred_element_type=F32)
            out_ref[0] = both[:size].astype(BF16)
            out_ref[1] = both[size:].astype(BF16)

    outs = [struct((2, size, wide), BF16)] * slabs
    flops = 8 * size * ny * ny
    return call(body, outs, [green, total, table_y, *arrays], [pltpu.VMEM((2 * size, 2 * ny), BF16)], flops, "finish_rows")


def gather_rows(blocks, right_ref, size):
    wide = blocks[0].shape[2]
    half = len(blocks) * size
    for m, ref in enumerate(blocks):
        top, low = pl.ds(m * size, size), pl.ds(half + m * size, size)
        right_ref[top, pl.ds(0, wide)] = ref[0]
        right_ref[top, pl.ds(wide, wide)] = ref[1]
        right_ref[low, pl.ds(0, wide)] = -ref[1]
        right_ref[low, pl.ds(wide, wide)] = ref[0]


def transform_x(table_x, blocks, total=None, contrast=None):
    _, size, wide = blocks[0].shape
    nx = table_x.shape[1]
    half = len(blocks) * size
    tall = min(nx, 128)

    def body(table_ref, *refs):
        ins, (out_ref, right_ref) = refs[:-2], refs[-2:]
        gather_rows(ins[: len(blocks)], right_ref, size)
        for x in range(0, nx, tall):
            row = pl.ds(x, tall)
            part = jnp.dot(table_ref[0, row, :], right_ref[pl.ds(0, half), :], preferred_element_type=F32)
            part += jnp.dot(table_ref[1, row, :], right_ref[pl.ds(half, half), :], preferred_element_type=F32)
            if contrast is None:
                out_ref[row, :] = part
            else:
                total_ref, contrast_ref = ins[len(blocks) :]
                part += total_ref[row, :]
                scale = contrast_ref[row, :]
                out_ref[0, row, :] = (part[:, :wide] * scale).astype(BF16)
                out_ref[1, row, :] = (part[:, wide:] * scale).astype(BF16)

    scratch = [pltpu.VMEM((2 * half, 2 * wide), BF16)]
    flops = 8 * nx * half * wide
    if contrast is None:
        return call(body, [struct((nx, 2 * wide), F32)], [table_x, *blocks], scratch, flops, "transform_x")[0]
    out = struct((2, nx, wide), BF16)
    spec = pl.BlockSpec(memory_space=pltpu.VMEM)
    ins = [table_x, *blocks, total, contrast]
    return pl.pallas_call(
        body,
        out_shape=out,
        in_specs=[spec] * len(ins),
        out_specs=spec,
        scratch_shapes=scratch,
        compiler_params=pltpu.CompilerParams(vmem_limit_bytes=24 * MIB),
        cost_estimate=pl.CostEstimate(flops=flops, bytes_accessed=4 * MIB, transcendentals=0),
        name="transform_x_last",
    )(*[in_vmem(v) for v in ins])


def on_cube_device(slabs, spectra, green, contrast):
    _, _, kx_dev, ny = spectra.shape
    nx = contrast.shape[1]
    parts = [(0, kx_dev // 2), (kx_dev // 2, kx_dev // 2)]
    own, green, contrast = spectra[0], green[0], contrast[0]

    def pairs(f):
        return [(i, f(i)) for i in range(8)]

    swap = pairs(lambda i: i ^ 1)
    first = pairs(lambda i: i ^ 2 if i % 2 == 0 else i ^ 4)
    second = pairs(lambda i: i ^ 4 if i % 2 == 0 else i ^ 2)

    def send(v, route):
        return lax.ppermute(v, "depth", route)

    def layers(masks):
        def at():
            me = lax.axis_index("depth")
            c = lax.rem(me, 2)
            return [jnp.bitwise_xor(me, jnp.where(c == 0, m0, m1)) for m0, m1 in masks]

        return at

    near = send(own, first)
    far = [send(own[:, s : s + n], second) for s, n in parts]
    own_swap = send(own, swap)
    table_y, *table_x = tables(nx, ny, kx_dev, parts, slabs)
    near_swap = send(near, swap)
    across = [send(near[:, s : s + n], second) for s, n in parts]
    total = first_sum(green, [own, own_swap, near, near_swap], layers([(0, 0), (1, 1), (2, 4), (5, 3)]))
    field = None
    for i, (start, size) in enumerate(parts):
        far_swap, across_swap = send(far[i], swap), send(across[i], swap)
        halves = finish_rows(
            green, total, [far[i], far_swap, across[i], across_swap], layers([(4, 2), (3, 5), (6, 6), (7, 7)]),
            table_y, start, slabs,
        )
        blocks = [halves[0]]
        for m in range(1, slabs):
            blocks.append(lax.ppermute(halves[m], "kslab", [(k, k ^ m) for k in range(slabs)]))
        if i < len(parts) - 1:
            field = transform_x(table_x[i], blocks)
        else:
            field = transform_x(table_x[i], blocks, field, contrast)
    return field[None]


def solution(mesh):
    in_specs = (
        P("depth", None, "kslab", None),
        P("depth", None, None, "kslab", None),
        P("depth", None, "kslab"),
    )
    out_specs = P("depth", None, None, "kslab")
    depth, slabs = mesh.shape["depth"], mesh.shape["kslab"]

    def on_device(spectra, green, contrast):
        cube = depth == 8 and spectra.shape[0] == 1 and slabs & (slabs - 1) == 0
        if cube and spectra.shape[2] % 64 == 0 and (spectra.shape[3] // slabs) % 128 == 0:
            return on_cube_device(slabs, spectra, green, contrast)
        return on_any_device(spectra, green, contrast)

    return jax.shard_map(on_device, mesh=mesh, in_specs=in_specs, out_specs=out_specs, check_vma=False)
```

```python
import math

import jax
import jax.numpy as jnp
from jax import lax
from jax.experimental import pallas as pl
from jax.experimental.pallas import tpu as pltpu
from jax.sharding import PartitionSpec as P


F32 = jnp.float32
BF16 = jnp.bfloat16
ROWS = 16
FINE = 32
MIB = 1 << 20


def fourier_tables(length):
    indices = jnp.arange(length, dtype=jnp.int32)
    products = indices[:, None] * indices[None, :] % length
    angles = products.astype(F32) * (2.0 * math.pi / length)
    factor = 1.0 / math.sqrt(length)
    return (jnp.cos(angles) * factor).astype(BF16), (jnp.sin(angles) * factor).astype(BF16)


def on_any_device(spectra, green, contrast):
    lay_dev, _, kx_dev, ny = spectra.shape
    nx = contrast.shape[1]
    coeffs = green.astype(F32)
    sources = lax.all_gather(spectra, "depth", axis=0, tiled=True).astype(F32)[None]
    real_part = jnp.sum(coeffs[:, :, 0] * sources[:, :, 0] - coeffs[:, :, 1] * sources[:, :, 1], axis=1)
    imag_part = jnp.sum(coeffs[:, :, 0] * sources[:, :, 1] + coeffs[:, :, 1] * sources[:, :, 0], axis=1)
    rounded = jnp.stack([real_part, imag_part], axis=1).astype(BF16)
    table_y = jnp.concatenate(fourier_tables(ny), axis=1)
    rows = lay_dev * kx_dev
    from_real = jnp.dot(rounded[:, 0].reshape(rows, ny), table_y, preferred_element_type=F32)
    from_imag = jnp.dot(rounded[:, 1].reshape(rows, ny), table_y, preferred_element_type=F32)
    halfway_real = (from_real[:, :ny] - from_imag[:, ny:]).reshape(lay_dev, kx_dev, ny)
    halfway_imag = (from_real[:, ny:] + from_imag[:, :ny]).reshape(lay_dev, kx_dev, ny)
    halfway = jnp.stack([halfway_real, halfway_imag], axis=1).astype(BF16)
    table_x = jnp.concatenate(fourier_tables(nx), axis=0)
    stacked = jnp.einsum(
        "ak,nckd->ncad",
        table_x,
        lax.all_to_all(halfway, "kslab", split_axis=3, concat_axis=2, tiled=True),
        preferred_element_type=F32,
    )
    real_part = stacked[:, 0, :nx] - stacked[:, 1, nx:]
    imag_part = stacked[:, 0, nx:] + stacked[:, 1, :nx]
    return (jnp.stack([real_part, imag_part], axis=1) * contrast[:, None]).astype(BF16)


def in_vmem(x):
    return pltpu.with_memory_space_constraint(x, pltpu.VMEM)


def call(body, outs, ins, scratch=(), flops=0, vmem=24 * MIB):
    spec = pl.BlockSpec(memory_space=pltpu.VMEM)
    moved = sum(math.prod(v.shape) * v.dtype.itemsize for v in list(outs) + list(ins))
    return pl.pallas_call(
        body,
        out_shape=[pltpu.VMEM(o.shape, o.dtype) for o in outs],
        in_specs=[spec] * len(ins),
        out_specs=[spec] * len(outs),
        scratch_shapes=list(scratch),
        compiler_params=pltpu.CompilerParams(vmem_limit_bytes=vmem),
        cost_estimate=pl.CostEstimate(flops=flops, bytes_accessed=moved, transcendentals=0),
    )(*[in_vmem(v) for v in ins])


def struct(shape, dtype):
    return jax.ShapeDtypeStruct(shape, dtype)


def modulo(v, length):
    return v & (length - 1) if length & (length - 1) == 0 else lax.rem(v, length)


def fill_table(length, columns, coarse_ref, put):
    width = columns.shape[1]
    step = 2.0 * math.pi / length
    factor = 1.0 / math.sqrt(length)
    rows = lax.broadcasted_iota(jnp.int32, (length // FINE, width), 0) * FINE
    angle = modulo(rows * columns, length).astype(F32) * step
    coarse_ref[0, pl.ds(0, length // FINE)] = jnp.cos(angle) * factor
    coarse_ref[1, pl.ds(0, length // FINE)] = jnp.sin(angle) * factor
    rows = lax.broadcasted_iota(jnp.int32, (FINE, width), 0)
    angle = modulo(rows * columns, length).astype(F32) * step
    coarse_ref[2, pl.ds(0, FINE)] = jnp.cos(angle)
    coarse_ref[3, pl.ds(0, FINE)] = jnp.sin(angle)

    @pl.loop(0, length // FINE)
    def _(block):
        for left in range(0, width, 256):
            cols = pl.ds(left, min(256, width - left))
            cos_c, sin_c = coarse_ref[0, pl.ds(block, 1), cols], coarse_ref[1, pl.ds(block, 1), cols]
            cos_f, sin_f = coarse_ref[2, pl.ds(0, FINE), cols], coarse_ref[3, pl.ds(0, FINE), cols]
            row = pl.ds(pl.multiple_of(block * FINE, FINE), FINE)
            put(row, left, cols, cos_c * cos_f - sin_c * sin_f, sin_c * cos_f + cos_c * sin_f)


def split_rows(own, parts):
    planes, _, ny = own.shape

    def body(own_ref, *refs):
        outs, sems = refs[:-1], refs[-1]
        copies = [
            pltpu.make_async_copy(own_ref.at[:, pl.ds(start, size)], ref, sems.at[i])
            for i, ((start, size), ref) in enumerate(zip(parts, outs))
        ]
        for copy in copies:
            copy.start()
        for copy in copies:
            copy.wait()

    return pl.pallas_call(
        body,
        out_shape=[pltpu.VMEM((planes, size, ny), own.dtype) for _, size in parts],
        in_specs=[pl.BlockSpec(memory_space=pl.ANY)],
        out_specs=[pl.BlockSpec(memory_space=pltpu.VMEM)] * len(parts),
        scratch_shapes=[pltpu.SemaphoreType.DMA((len(parts),))],
        compiler_params=pltpu.CompilerParams(vmem_limit_bytes=8 * MIB),
        cost_estimate=pl.CostEstimate(flops=0, bytes_accessed=MIB, transcendentals=0),
        name="split_rows",
    )(pltpu.with_memory_space_constraint(own, pltpu.HBM))


def prepare(green, contrast, kx_dev, parts, slabs):
    ny, nx = green.shape[3], contrast.shape[0]
    args = [green, contrast]

    def body(*refs):
        given, (ty_ref, *tx_refs) = refs[:2], refs[2 : 3 + len(parts)]
        kept, (coarse_y, coarse_x, sems) = refs[3 + len(parts) : -3], refs[-3:]
        copies = [pltpu.make_async_copy(a, b, sems.at[i]) for i, (a, b) in enumerate(zip(given, kept))]
        for copy in copies:
            copy.start()
        z = lax.axis_index("kslab")
        wide = ny // slabs
        lane = lax.broadcasted_iota(jnp.int32, (1, ny), 1)
        columns = jnp.bitwise_xor(lane // wide, z) * wide + lane % wide

        def put_y(row, left, cols, cos, sin):
            ty_ref[0, row, cols] = cos.astype(BF16)
            ty_ref[1, row, cols] = sin.astype(BF16)

        fill_table(ny, columns, coarse_y, put_y)
        for (start, size), tx_ref in zip(parts, tx_refs):
            lane = lax.broadcasted_iota(jnp.int32, (1, slabs * size), 1)
            columns = jnp.bitwise_xor(lane // size, z) * kx_dev + start + lane % size

            def put_x(row, left, cols, cos, sin):
                tx_ref[0, row, cols] = cos.astype(BF16)
                tx_ref[1, row, cols] = sin.astype(BF16)

            fill_table(nx, columns, coarse_x.at[:, :, pl.ds(0, slabs * size)], put_x)
        for copy in copies:
            copy.wait()

    outs = [struct((2, ny, ny), BF16)]
    outs += [struct((2, nx, slabs * size), BF16) for _, size in parts]
    outs += [struct(v.shape, v.dtype) for v in args]
    most = max(size for _, size in parts)
    anywhere, vmem = pl.BlockSpec(memory_space=pl.ANY), pl.BlockSpec(memory_space=pltpu.VMEM)
    made = pl.pallas_call(
        body,
        out_shape=[pltpu.VMEM(o.shape, o.dtype) for o in outs],
        in_specs=[anywhere] * 2,
        out_specs=[vmem] * len(outs),
        scratch_shapes=[
            pltpu.VMEM((4, max(ny // FINE, FINE), ny), F32),
            pltpu.VMEM((4, max(nx // FINE, FINE), slabs * most), F32),
            pltpu.SemaphoreType.DMA((2,)),
        ],
        compiler_params=pltpu.CompilerParams(vmem_limit_bytes=24 * MIB),
        cost_estimate=pl.CostEstimate(flops=8 * ny * ny, bytes_accessed=8 * MIB, transcendentals=0),
        name="prepare",
    )(*[pltpu.with_memory_space_constraint(v, pltpu.HBM) for v in args])
    return made[0], made[1 : 1 + len(parts)], made[1 + len(parts) :]


def add_sources(total, green_ref, sources, step, start, cols):
    real, imag = total
    whole = pl.ds(pl.multiple_of(start + step * ROWS, ROWS), ROWS)
    for ref, at, layer in sources:
        row = pl.ds(pl.multiple_of(at + step * ROWS, ROWS), ROWS)
        g_real, g_imag = green_ref[layer, 0, whole, cols].astype(F32), green_ref[layer, 1, whole, cols].astype(F32)
        s_real, s_imag = ref[0, row, cols].astype(F32), ref[1, row, cols].astype(F32)
        p_real = g_real * s_real - g_imag * s_imag
        p_imag = g_real * s_imag + g_imag * s_real
        real = p_real if real is None else real + p_real
        imag = p_imag if imag is None else imag + p_imag
    return real, imag


def early_sum(green, arrays, offsets, layers, start, size):
    ny = arrays[0].shape[2]

    def body(green_ref, *refs):
        total_ref = refs[-1]
        sources = list(zip(refs[:-1], offsets, layers()))

        @pl.loop(0, size // ROWS)
        def _(step):
            row = pl.ds(pl.multiple_of(step * ROWS, ROWS), ROWS)
            for left in range(0, ny, 256):
                cols = pl.ds(left, 256)
                total_ref[0, row, cols], total_ref[1, row, cols] = add_sources(
                    (None, None), green_ref, sources, step, start, cols
                )

    return call(body, [struct((2, size, ny), F32)], [green, *arrays], flops=8 * len(arrays) * size * ny)[0]


def finish_rows(green, total, arrays, layers, table_y, start, slabs, groups):
    _, size, ny = arrays[0].shape
    wide = ny // slabs

    def body(green_ref, total_ref, table_ref, *refs):
        ins, outs, left_ref = refs[: len(arrays)], refs[len(arrays) : -1], refs[-1]
        sources = [(ref, 0, layer) for ref, layer in zip(ins, layers())]

        @pl.loop(0, size // ROWS)
        def _(step):
            row = pl.ds(pl.multiple_of(step * ROWS, ROWS), ROWS)
            low = pl.ds(pl.multiple_of(size + step * ROWS, ROWS), ROWS)
            for left in range(0, ny, 256):
                cols = pl.ds(left, 256)
                begun = total_ref[0, row, cols], total_ref[1, row, cols]
                real, imag = add_sources(begun, green_ref, sources, step, start, cols)
                left_ref[row, pl.ds(left, 256)] = real.astype(BF16)
                left_ref[row, pl.ds(ny + left, 256)] = (-imag).astype(BF16)
                left_ref[low, pl.ds(left, 256)] = imag.astype(BF16)
                left_ref[low, pl.ds(ny + left, 256)] = real.astype(BF16)

        for group, out_ref in zip(groups, outs):
            for i, m in enumerate(group):
                cols = pl.ds(m * wide, wide)
                both = jnp.dot(left_ref[:, pl.ds(0, ny)], table_ref[0, :, cols], preferred_element_type=F32)
                both += jnp.dot(left_ref[:, pl.ds(ny, ny)], table_ref[1, :, cols], preferred_element_type=F32)
                out_ref[2 * i] = both[:size].astype(BF16)
                out_ref[2 * i + 1] = both[size:].astype(BF16)

    outs = [struct((2 * len(group), size, wide), BF16) for group in groups]
    flops = 8 * size * ny * ny
    return call(body, outs, [green, total, table_y, *arrays], [pltpu.VMEM((2 * size, 2 * ny), BF16)], flops)


def second_half(pair):
    count = pair.shape[0] // 2

    def body(pair_ref, out_ref):
        out_ref[...] = pair_ref[count:]

    return call(body, [struct((count, *pair.shape[1:]), pair.dtype)], [pair])[0]


def transform_x(table_x, blocks, size, total=None, contrast=None):
    arrays = []
    for array, _ in blocks:
        if not any(array is other for other in arrays):
            arrays.append(array)
    at = [next(i for i, other in enumerate(arrays) if other is array) for array, _ in blocks]
    wide = arrays[0].shape[2]
    nx = table_x.shape[1]
    half = len(blocks) * size
    tall = min(nx, 128)

    def fill(ins, right_ref):
        for m, (_, place) in enumerate(blocks):
            real, imag = ins[at[m]][place], ins[at[m]][place + 1]
            top, low = pl.ds(m * size, size), pl.ds(half + m * size, size)
            right_ref[top, pl.ds(0, wide)] = real
            right_ref[top, pl.ds(wide, wide)] = imag
            right_ref[low, pl.ds(0, wide)] = -imag
            right_ref[low, pl.ds(wide, wide)] = real

    def product(table_ref, right_ref, row):
        part = jnp.dot(table_ref[0, row, :], right_ref[pl.ds(0, half), :], preferred_element_type=F32)
        return part + jnp.dot(table_ref[1, row, :], right_ref[pl.ds(half, half), :], preferred_element_type=F32)

    def body(table_ref, *refs):
        ins, (out_ref, right_ref) = refs[:-2], refs[-2:]
        fill(ins, right_ref)
        for x in range(0, nx, tall):
            row = pl.ds(x, tall)
            part = product(table_ref, right_ref, row)
            out_ref[row, :] = part if total is None else part + ins[-1][row, :]

    def last_body(table_ref, *refs):
        ins, (out_ref, right_ref, kept_ref, sems) = refs[:-4], refs[-4:]
        total_ref, contrast_ref = ins[-2:]
        fill(ins, right_ref)
        copies = []
        for i, x in enumerate(range(0, nx, tall)):
            row = pl.ds(x, tall)
            part = product(table_ref, right_ref, row) + total_ref[row, :]
            scale = contrast_ref[row, :]
            kept_ref[0, row, :] = (part[:, :wide] * scale).astype(BF16)
            kept_ref[1, row, :] = (part[:, wide:] * scale).astype(BF16)
            copies.append(pltpu.make_async_copy(kept_ref.at[:, row], out_ref.at[:, row], sems.at[i]))
            copies[-1].start()
        for copy in copies:
            copy.wait()

    scratch = [pltpu.VMEM((2 * half, 2 * wide), BF16)]
    flops = 8 * nx * half * wide
    if contrast is None:
        ins = [table_x, *arrays] + ([] if total is None else [total])
        return call(body, [struct((nx, 2 * wide), F32)], ins, scratch, flops)[0]
    ins = [table_x, *arrays, total, contrast]
    return pl.pallas_call(
        last_body,
        out_shape=struct((2, nx, wide), BF16),
        in_specs=[pl.BlockSpec(memory_space=pltpu.VMEM)] * len(ins),
        out_specs=pl.BlockSpec(memory_space=pl.ANY),
        scratch_shapes=scratch + [pltpu.VMEM((2, nx, wide), BF16), pltpu.SemaphoreType.DMA((nx // tall,))],
        compiler_params=pltpu.CompilerParams(vmem_limit_bytes=24 * MIB),
        cost_estimate=pl.CostEstimate(flops=flops, bytes_accessed=4 * MIB, transcendentals=0),
        name="transform_x_last",
    )(*[in_vmem(v) for v in ins])


def on_cube_device(slabs, spectra, green, contrast):
    _, _, kx_dev, _ = spectra.shape
    parts = [(0, kx_dev // 2), (kx_dev // 2, kx_dev // 2)]
    own, green, contrast = spectra[0], green[0], contrast[0]

    swap = [(i, i ^ 1) for i in range(8)]
    out = [(i, i ^ 2 if i % 2 == 0 else i ^ 4) for i in range(8)]

    def send(v, route):
        return lax.ppermute(v, "depth", route)

    def layers(masks):
        def at():
            me = lax.axis_index("depth")
            c = lax.rem(me, 2)
            return [jnp.bitwise_xor(me, jnp.where(c == 0, m0, m1)) for m0, m1 in masks]

        return at

    owns = split_rows(own, parts)
    near = [send(v, out) for v in owns]
    own_swap = send(own, swap)
    table_y, table_x, (green, contrast) = prepare(green, contrast, kx_dev, parts, slabs)
    near_swap = [send(v, swap) for v in near]
    far = [send(own_swap[:, s : s + n], out) for s, n in parts]
    across = [send(v, out) for v in near_swap]
    field = None
    results = []
    for i, (start, size) in enumerate(parts):
        far_swap, across_swap = send(far[i], swap), send(across[i], swap)
        total = early_sum(
            green, [owns[i], own_swap, near[i], near_swap[i], far[i], far_swap], [0, start, 0, 0, 0, 0],
            layers([(0, 0), (1, 1), (2, 4), (5, 3), (3, 5), (4, 2)]), start, size,
        )
        relay = slabs == 4 and i < len(parts) - 1
        groups = [[0], [1], [2, 3]] if relay else [[m] for m in range(slabs)]
        halves = finish_rows(
            green, total, [across[i], across_swap], layers([(7, 7), (6, 6)]), table_y, start, slabs, groups
        )

        def hop(m, v):
            return lax.ppermute(v, "kslab", [(k, k ^ m) for k in range(slabs)])

        if relay:
            two, one = hop(2, halves[2]), hop(1, halves[1])
            results.append([(halves[0], 0), (one, 0), (two, 0), (two, 2)])
        else:
            results.append([(halves[0], 0)] + [(hop(m, halves[m]), 0) for m in range(1, slabs)])
    for result in results[:-1]:
        if slabs == 4:
            passed = second_half(result[3][0])
            result[3] = (lax.ppermute(passed, "kslab", [(k, k ^ 1) for k in range(slabs)]), 0)
    for i, (start, size) in enumerate(parts):
        field = transform_x(table_x[i], results[i], size, field, contrast if i == len(parts) - 1 else None)
    return field[None]


def solution(mesh):
    in_specs = (
        P("depth", None, "kslab", None),
        P("depth", None, None, "kslab", None),
        P("depth", None, "kslab"),
    )
    out_specs = P("depth", None, None, "kslab")
    depth, slabs = mesh.shape["depth"], mesh.shape["kslab"]

    def on_device(spectra, green, contrast):
        cube = depth == 8 and spectra.shape[0] == 1 and slabs & (slabs - 1) == 0
        if cube and spectra.shape[2] % 64 == 0 and (spectra.shape[3] // slabs) % 128 == 0:
            return on_cube_device(slabs, spectra, green, contrast)
        return on_any_device(spectra, green, contrast)

    return jax.shard_map(on_device, mesh=mesh, in_specs=in_specs, out_specs=out_specs, check_vma=False)
```

```python
import math

import jax
import jax.numpy as jnp
from jax import lax
from jax.experimental import pallas as pl
from jax.experimental.pallas import tpu as pltpu
from jax.sharding import PartitionSpec as P


F32 = jnp.float32
BF16 = jnp.bfloat16
ROWS = 16
FINE = 32
MIB = 1 << 20


def fourier_tables(length):
    indices = jnp.arange(length, dtype=jnp.int32)
    products = indices[:, None] * indices[None, :] % length
    angles = products.astype(F32) * (2.0 * math.pi / length)
    factor = 1.0 / math.sqrt(length)
    return (jnp.cos(angles) * factor).astype(BF16), (jnp.sin(angles) * factor).astype(BF16)


def on_any_device(spectra, green, contrast):
    lay_dev, _, kx_dev, ny = spectra.shape
    nx = contrast.shape[1]
    coeffs = green.astype(F32)
    sources = lax.all_gather(spectra, "depth", axis=0, tiled=True).astype(F32)[None]
    real_part = jnp.sum(coeffs[:, :, 0] * sources[:, :, 0] - coeffs[:, :, 1] * sources[:, :, 1], axis=1)
    imag_part = jnp.sum(coeffs[:, :, 0] * sources[:, :, 1] + coeffs[:, :, 1] * sources[:, :, 0], axis=1)
    rounded = jnp.stack([real_part, imag_part], axis=1).astype(BF16)
    table_y = jnp.concatenate(fourier_tables(ny), axis=1)
    rows = lay_dev * kx_dev
    from_real = jnp.dot(rounded[:, 0].reshape(rows, ny), table_y, preferred_element_type=F32)
    from_imag = jnp.dot(rounded[:, 1].reshape(rows, ny), table_y, preferred_element_type=F32)
    halfway_real = (from_real[:, :ny] - from_imag[:, ny:]).reshape(lay_dev, kx_dev, ny)
    halfway_imag = (from_real[:, ny:] + from_imag[:, :ny]).reshape(lay_dev, kx_dev, ny)
    halfway = jnp.stack([halfway_real, halfway_imag], axis=1).astype(BF16)
    table_x = jnp.concatenate(fourier_tables(nx), axis=0)
    stacked = jnp.einsum(
        "ak,nckd->ncad",
        table_x,
        lax.all_to_all(halfway, "kslab", split_axis=3, concat_axis=2, tiled=True),
        preferred_element_type=F32,
    )
    real_part = stacked[:, 0, :nx] - stacked[:, 1, nx:]
    imag_part = stacked[:, 0, nx:] + stacked[:, 1, :nx]
    return (jnp.stack([real_part, imag_part], axis=1) * contrast[:, None]).astype(BF16)


def in_vmem(x):
    return pltpu.with_memory_space_constraint(x, pltpu.VMEM)


def call(body, outs, ins, scratch=(), flops=0, vmem=24 * MIB):
    spec = pl.BlockSpec(memory_space=pltpu.VMEM)
    moved = sum(math.prod(v.shape) * v.dtype.itemsize for v in list(outs) + list(ins))
    return pl.pallas_call(
        body,
        out_shape=[pltpu.VMEM(o.shape, o.dtype) for o in outs],
        in_specs=[spec] * len(ins),
        out_specs=[spec] * len(outs),
        scratch_shapes=list(scratch),
        compiler_params=pltpu.CompilerParams(vmem_limit_bytes=vmem),
        cost_estimate=pl.CostEstimate(flops=flops, bytes_accessed=moved, transcendentals=0),
    )(*[in_vmem(v) for v in ins])


def struct(shape, dtype):
    return jax.ShapeDtypeStruct(shape, dtype)


def modulo(v, length):
    return v & (length - 1) if length & (length - 1) == 0 else lax.rem(v, length)


def fill_table(length, columns, coarse_ref, put):
    width = columns.shape[1]
    unit = 2.0 * math.pi / length
    factor = 1.0 / math.sqrt(length)
    rows = lax.broadcasted_iota(jnp.int32, (length // FINE, width), 0) * FINE
    angle = modulo(rows * columns, length).astype(F32) * unit
    coarse_ref[0, pl.ds(0, length // FINE)] = jnp.cos(angle) * factor
    coarse_ref[1, pl.ds(0, length // FINE)] = jnp.sin(angle) * factor
    rows = lax.broadcasted_iota(jnp.int32, (FINE, width), 0)
    angle = modulo(rows * columns, length).astype(F32) * unit
    coarse_ref[2, pl.ds(0, FINE)] = jnp.cos(angle)
    coarse_ref[3, pl.ds(0, FINE)] = jnp.sin(angle)

    @pl.loop(0, length // FINE)
    def _(block):
        step = 256 if width % 256 == 0 else width
        for left in range(0, width, step):
            cols = pl.ds(left, step)
            cos_c, sin_c = coarse_ref[0, pl.ds(block, 1), cols], coarse_ref[1, pl.ds(block, 1), cols]
            cos_f, sin_f = coarse_ref[2, pl.ds(0, FINE), cols], coarse_ref[3, pl.ds(0, FINE), cols]
            row = pl.ds(pl.multiple_of(block * FINE, FINE), FINE)
            put(row, left, cols, cos_c * cos_f - sin_c * sin_f, sin_c * cos_f + cos_c * sin_f)


def split_rows(own, parts):
    planes, _, ny = own.shape

    def body(own_ref, *refs):
        outs, sems = refs[:-1], refs[-1]
        copies = [
            pltpu.make_async_copy(own_ref.at[:, pl.ds(start, size)], ref, sems.at[i])
            for i, ((start, size), ref) in enumerate(zip(parts, outs))
        ]
        for copy in copies:
            copy.start()
        for copy in copies:
            copy.wait()

    return pl.pallas_call(
        body,
        out_shape=[pltpu.VMEM((planes, size, ny), own.dtype) for _, size in parts],
        in_specs=[pl.BlockSpec(memory_space=pl.ANY)],
        out_specs=[pl.BlockSpec(memory_space=pltpu.VMEM)] * len(parts),
        scratch_shapes=[pltpu.SemaphoreType.DMA((len(parts),))],
        compiler_params=pltpu.CompilerParams(vmem_limit_bytes=8 * MIB),
        cost_estimate=pl.CostEstimate(flops=0, bytes_accessed=MIB, transcendentals=0),
        name="split_rows",
    )(pltpu.with_memory_space_constraint(own, pltpu.HBM))


def prepare(green, contrast, kx_dev, columns_of, slabs):
    ny, nx = green.shape[3], contrast.shape[0]
    args = [green, contrast]

    def body(*refs):
        given, (ty_ref, *tx_refs) = refs[:2], refs[2 : 3 + len(columns_of)]
        count = len(columns_of)
        kept, (coarse_y, *coarse_x, sems) = refs[3 + count : -2 - count], refs[-2 - count :]
        copies = [pltpu.make_async_copy(a, b, sems.at[i]) for i, (a, b) in enumerate(zip(given, kept))]
        for copy in copies:
            copy.start()
        z = lax.axis_index("kslab")
        wide = ny // slabs
        lane = lax.broadcasted_iota(jnp.int32, (1, ny), 1)
        columns = lax.rem(lane // wide + z, slabs) * wide + lane % wide

        def put_y(row, left, cols, cos, sin):
            ty_ref[0, row, cols] = cos.astype(BF16)
            ty_ref[1, row, cols] = sin.astype(BF16)

        fill_table(ny, columns, coarse_y, put_y)
        for blocks, tx_ref, coarse_ref in zip(columns_of, tx_refs, coarse_x):
            total = tx_ref.shape[2]
            lane = lax.broadcasted_iota(jnp.int32, (1, total), 1)
            columns, at = lane, 0
            for m, start, size in blocks:
                here = lax.rem(z + slabs - m, slabs) * kx_dev + start - at + lane
                columns, at = jnp.where(lane >= at, here, columns), at + size

            def put_x(row, left, cols, cos, sin):
                tx_ref[0, row, cols] = cos.astype(BF16)
                tx_ref[1, row, cols] = sin.astype(BF16)

            fill_table(nx, columns, coarse_ref, put_x)
        for copy in copies:
            copy.wait()

    outs = [struct((2, ny, ny), BF16)]
    widths = [-(-sum(size for _, _, size in blocks) // 128) * 128 for blocks in columns_of]
    outs += [struct((2, nx, width), BF16) for width in widths]
    outs += [struct(v.shape, v.dtype) for v in args]
    anywhere, vmem = pl.BlockSpec(memory_space=pl.ANY), pl.BlockSpec(memory_space=pltpu.VMEM)
    made = pl.pallas_call(
        body,
        out_shape=[pltpu.VMEM(o.shape, o.dtype) for o in outs],
        in_specs=[anywhere] * 2,
        out_specs=[vmem] * len(outs),
        scratch_shapes=[
            pltpu.VMEM((4, max(ny // FINE, FINE), ny), F32),
            *[pltpu.VMEM((4, max(nx // FINE, FINE), width), F32) for width in widths],
            pltpu.SemaphoreType.DMA((2,)),
        ],
        compiler_params=pltpu.CompilerParams(vmem_limit_bytes=24 * MIB),
        cost_estimate=pl.CostEstimate(flops=8 * ny * ny, bytes_accessed=8 * MIB, transcendentals=0),
        name="prepare",
    )(*[pltpu.with_memory_space_constraint(v, pltpu.HBM) for v in args])
    return made[0], made[1 : 1 + len(widths)], made[1 + len(widths) :]


def add_sources(total, green_ref, sources, step, start, cols):
    real, imag = total
    whole = pl.ds(pl.multiple_of(start + step * ROWS, ROWS), ROWS)
    for ref, plane, at, layer in sources:
        row = pl.ds(pl.multiple_of(at + step * ROWS, ROWS), ROWS)
        g_real, g_imag = green_ref[layer, 0, whole, cols].astype(F32), green_ref[layer, 1, whole, cols].astype(F32)
        s_real, s_imag = ref[plane, row, cols].astype(F32), ref[plane + 1, row, cols].astype(F32)
        p_real = g_real * s_real - g_imag * s_imag
        p_imag = g_real * s_imag + g_imag * s_real
        real = p_real if real is None else real + p_real
        imag = p_imag if imag is None else imag + p_imag
    return real, imag


def unique(arrays):
    kept = []
    for array in arrays:
        if not any(array is other for other in kept):
            kept.append(array)
    return kept, [next(i for i, other in enumerate(kept) if other is array) for array in arrays]


def early_sum(green, sources, layers, start, size):
    arrays, at = unique([array for array, _, _ in sources])
    ny = arrays[0].shape[2]

    def body(green_ref, *refs):
        total_ref = refs[-1]
        given = [(refs[i], plane, row, layer) for i, (_, plane, row), layer in zip(at, sources, layers())]

        @pl.loop(0, size // ROWS)
        def _(step):
            row = pl.ds(pl.multiple_of(step * ROWS, ROWS), ROWS)
            for left in range(0, ny, 256):
                cols = pl.ds(left, 256)
                total_ref[0, row, cols], total_ref[1, row, cols] = add_sources(
                    (None, None), green_ref, given, step, start, cols
                )

    flops = 8 * len(sources) * size * ny
    return call(body, [struct((2, size, ny), F32)], [green, *arrays], flops=flops)[0]


def finish_rows(green, total, sources, layers, table_y, start, size, slabs):
    arrays, at = unique([array for array, _, _ in sources])
    ny = arrays[0].shape[2]
    wide = ny // slabs

    def body(green_ref, total_ref, table_ref, *refs):
        ins, outs, left_ref = refs[: len(arrays)], refs[len(arrays) : -1], refs[-1]
        given = [(ins[i], plane, row, layer) for i, (_, plane, row), layer in zip(at, sources, layers())]

        @pl.loop(0, size // ROWS)
        def _(step):
            row = pl.ds(pl.multiple_of(step * ROWS, ROWS), ROWS)
            low = pl.ds(pl.multiple_of(size + step * ROWS, ROWS), ROWS)
            for left in range(0, ny, 256):
                cols = pl.ds(left, 256)
                begun = total_ref[0, row, cols], total_ref[1, row, cols]
                real, imag = add_sources(begun, green_ref, given, step, start, cols)
                left_ref[row, pl.ds(left, 256)] = real.astype(BF16)
                left_ref[row, pl.ds(ny + left, 256)] = (-imag).astype(BF16)
                left_ref[low, pl.ds(left, 256)] = imag.astype(BF16)
                left_ref[low, pl.ds(ny + left, 256)] = real.astype(BF16)

        for m, out_ref in enumerate(outs):
            cols = pl.ds(m * wide, wide)
            both = jnp.dot(left_ref[:, pl.ds(0, ny)], table_ref[0, :, cols], preferred_element_type=F32)
            both += jnp.dot(left_ref[:, pl.ds(ny, ny)], table_ref[1, :, cols], preferred_element_type=F32)
            out_ref[0] = both[:size].astype(BF16)
            out_ref[1] = both[size:].astype(BF16)

    outs = [struct((2, size, wide), BF16)] * slabs
    flops = 8 * size * ny * ny
    return call(body, outs, [green, total, table_y, *arrays], [pltpu.VMEM((2 * size, 2 * ny), BF16)], flops)


def transform_x(table_x, blocks, total=None, contrast=None):
    wide = blocks[0].shape[2]
    _, nx, half = table_x.shape
    tall = min(nx, 128)

    def fill(ins, right_ref):
        start = 0
        for ref in ins[: len(blocks)]:
            real, imag, size = ref[0], ref[1], ref.shape[1]
            top, low = pl.ds(start, size), pl.ds(half + start, size)
            right_ref[top, pl.ds(0, wide)] = real
            right_ref[top, pl.ds(wide, wide)] = imag
            right_ref[low, pl.ds(0, wide)] = -imag
            right_ref[low, pl.ds(wide, wide)] = real
            start += size
        if start < half:
            none = jnp.zeros((half - start, 2 * wide), BF16)
            right_ref[pl.ds(start, half - start), :] = none
            right_ref[pl.ds(half + start, half - start), :] = none

    def product(table_ref, right_ref, row):
        part = jnp.dot(table_ref[0, row, :], right_ref[pl.ds(0, half), :], preferred_element_type=F32)
        return part + jnp.dot(table_ref[1, row, :], right_ref[pl.ds(half, half), :], preferred_element_type=F32)

    def body(table_ref, *refs):
        ins, (out_ref, right_ref) = refs[:-2], refs[-2:]
        fill(ins, right_ref)
        for x in range(0, nx, tall):
            row = pl.ds(x, tall)
            part = product(table_ref, right_ref, row)
            out_ref[row, :] = part if total is None else part + ins[-1][row, :]

    def last_body(table_ref, *refs):
        ins, (out_ref, right_ref, kept_ref, sems) = refs[:-4], refs[-4:]
        total_ref, contrast_ref = ins[-2:]
        fill(ins, right_ref)
        copies = []
        for i, x in enumerate(range(0, nx, tall)):
            row = pl.ds(x, tall)
            part = product(table_ref, right_ref, row) + total_ref[row, :]
            scale = contrast_ref[row, :]
            kept_ref[0, row, :] = (part[:, :wide] * scale).astype(BF16)
            kept_ref[1, row, :] = (part[:, wide:] * scale).astype(BF16)
            copies.append(pltpu.make_async_copy(kept_ref.at[:, row], out_ref.at[:, row], sems.at[i]))
            copies[-1].start()
        for copy in copies:
            copy.wait()

    scratch = [pltpu.VMEM((2 * half, 2 * wide), BF16)]
    flops = 8 * nx * half * wide
    if contrast is None:
        ins = [table_x, *blocks] + ([] if total is None else [total])
        return call(body, [struct((nx, 2 * wide), F32)], ins, scratch, flops)[0]
    ins = [table_x, *blocks, total, contrast]
    return pl.pallas_call(
        last_body,
        out_shape=struct((2, nx, wide), BF16),
        in_specs=[pl.BlockSpec(memory_space=pltpu.VMEM)] * len(ins),
        out_specs=pl.BlockSpec(memory_space=pl.ANY),
        scratch_shapes=scratch + [pltpu.VMEM((2, nx, wide), BF16), pltpu.SemaphoreType.DMA((nx // tall,))],
        compiler_params=pltpu.CompilerParams(vmem_limit_bytes=24 * MIB),
        cost_estimate=pl.CostEstimate(flops=flops, bytes_accessed=4 * MIB, transcendentals=0),
        name="transform_x_last",
    )(*[in_vmem(v) for v in ins])


def on_cube_device(slabs, spectra, green, contrast):
    _, _, kx_dev, _ = spectra.shape
    parts = [(0, kx_dev // 2), (kx_dev // 2, kx_dev // 2)]
    own, green, contrast = spectra[0], green[0], contrast[0]

    swap = [(i, i ^ 1) for i in range(8)]
    out = [(i, i ^ 2 if i % 2 == 0 else i ^ 4) for i in range(8)]

    def send(v, route):
        return lax.ppermute(v, "depth", route)

    def layers(masks):
        def at():
            me = lax.axis_index("depth")
            c = lax.rem(me, 2)
            return [jnp.bitwise_xor(me, jnp.where(c == 0, m0, m1)) for m0, m1 in masks]

        return at

    owns = split_rows(own, parts)
    near = [send(v, out) for v in owns]
    own_swap = send(own, swap)
    columns_of = [[(m, start, size) for m in range(slabs)] for start, size in parts]
    table_y, table_x, (green, contrast) = prepare(green, contrast, kx_dev, columns_of, slabs)
    near_swap = [send(v, swap) for v in near]
    far = [send(own_swap[:, s : s + n], out) for s, n in parts]
    across = [send(v, out) for v in near_swap]

    def hop(m, v):
        return lax.ppermute(v, "kslab", [(k, (k + m) % slabs) for k in range(slabs)])

    halves = []
    for i, (start, size) in enumerate(parts):
        far_swap, across_swap = send(far[i], swap), send(across[i], swap)
        sources = [(owns[i], 0, 0), (own_swap, 0, start), (near[i], 0, 0), (near_swap[i], 0, 0), (far[i], 0, 0)]
        total = early_sum(green, sources, layers([(0, 0), (1, 1), (2, 4), (5, 3), (3, 5)]), start, size)
        sources = [(far_swap, 0, 0), (across[i], 0, 0), (across_swap, 0, 0)]
        halves.append(finish_rows(green, total, sources, layers([(4, 2), (7, 7), (6, 6)]), table_y, start, size, slabs))
    field = None
    for i, slab in enumerate(halves):
        blocks = [slab[0]] + [hop(m, slab[m]) for m in range(1, slabs)]
        field = transform_x(table_x[i], blocks, field, contrast if i == len(parts) - 1 else None)
    return field[None]


def solution(mesh):
    in_specs = (
        P("depth", None, "kslab", None),
        P("depth", None, None, "kslab", None),
        P("depth", None, "kslab"),
    )
    out_specs = P("depth", None, None, "kslab")
    depth, slabs = mesh.shape["depth"], mesh.shape["kslab"]

    def on_device(spectra, green, contrast):
        cube = depth == 8 and spectra.shape[0] == 1 and slabs == 4
        if cube and spectra.shape[2] % 128 == 0 and (spectra.shape[3] // slabs) % 128 == 0:
            return on_cube_device(slabs, spectra, green, contrast)
        return on_any_device(spectra, green, contrast)

    return jax.shard_map(on_device, mesh=mesh, in_specs=in_specs, out_specs=out_specs, check_vma=False)
```

```python
import math

import jax
import jax.numpy as jnp
from jax import lax
from jax.experimental import pallas as pl
from jax.experimental.pallas import tpu as pltpu
from jax.sharding import PartitionSpec as P


F32 = jnp.float32
BF16 = jnp.bfloat16
ROWS = 16
FINE = 32
MIB = 1 << 20
TALL = 128


def fourier_tables(length):
    indices = jnp.arange(length, dtype=jnp.int32)
    products = indices[:, None] * indices[None, :] % length
    angles = products.astype(F32) * (2.0 * math.pi / length)
    factor = 1.0 / math.sqrt(length)
    return (jnp.cos(angles) * factor).astype(BF16), (jnp.sin(angles) * factor).astype(BF16)


def on_any_device(spectra, green, contrast):
    lay_dev, _, kx_dev, ny = spectra.shape
    nx = contrast.shape[1]
    coeffs = green.astype(F32)
    sources = lax.all_gather(spectra, "depth", axis=0, tiled=True).astype(F32)[None]
    real_part = jnp.sum(coeffs[:, :, 0] * sources[:, :, 0] - coeffs[:, :, 1] * sources[:, :, 1], axis=1)
    imag_part = jnp.sum(coeffs[:, :, 0] * sources[:, :, 1] + coeffs[:, :, 1] * sources[:, :, 0], axis=1)
    rounded = jnp.stack([real_part, imag_part], axis=1).astype(BF16)
    table_y = jnp.concatenate(fourier_tables(ny), axis=1)
    rows = lay_dev * kx_dev
    from_real = jnp.dot(rounded[:, 0].reshape(rows, ny), table_y, preferred_element_type=F32)
    from_imag = jnp.dot(rounded[:, 1].reshape(rows, ny), table_y, preferred_element_type=F32)
    halfway_real = (from_real[:, :ny] - from_imag[:, ny:]).reshape(lay_dev, kx_dev, ny)
    halfway_imag = (from_real[:, ny:] + from_imag[:, :ny]).reshape(lay_dev, kx_dev, ny)
    halfway = jnp.stack([halfway_real, halfway_imag], axis=1).astype(BF16)
    table_x = jnp.concatenate(fourier_tables(nx), axis=0)
    stacked = jnp.einsum(
        "ak,nckd->ncad",
        table_x,
        lax.all_to_all(halfway, "kslab", split_axis=3, concat_axis=2, tiled=True),
        preferred_element_type=F32,
    )
    real_part = stacked[:, 0, :nx] - stacked[:, 1, nx:]
    imag_part = stacked[:, 0, nx:] + stacked[:, 1, :nx]
    return (jnp.stack([real_part, imag_part], axis=1) * contrast[:, None]).astype(BF16)


def in_vmem(x):
    return pltpu.with_memory_space_constraint(x, pltpu.VMEM)


def call(body, outs, ins, scratch=(), flops=0, vmem=24 * MIB):
    spec = pl.BlockSpec(memory_space=pltpu.VMEM)
    moved = sum(math.prod(v.shape) * v.dtype.itemsize for v in list(outs) + list(ins))
    return pl.pallas_call(
        body,
        out_shape=[pltpu.VMEM(o.shape, o.dtype) for o in outs],
        in_specs=[spec] * len(ins),
        out_specs=[spec] * len(outs),
        scratch_shapes=list(scratch),
        compiler_params=pltpu.CompilerParams(vmem_limit_bytes=vmem),
        cost_estimate=pl.CostEstimate(flops=flops, bytes_accessed=moved, transcendentals=0),
    )(*[in_vmem(v) for v in ins])


def struct(shape, dtype):
    return jax.ShapeDtypeStruct(shape, dtype)


def modulo(v, length):
    return v & (length - 1) if length & (length - 1) == 0 else lax.rem(v, length)


def fill_table(length, columns, coarse_ref, put):
    width = columns.shape[1]
    unit = 2.0 * math.pi / length
    factor = 1.0 / math.sqrt(length)
    rows = lax.broadcasted_iota(jnp.int32, (length // FINE, width), 0) * FINE
    angle = modulo(rows * columns, length).astype(F32) * unit
    coarse_ref[0, pl.ds(0, length // FINE)] = jnp.cos(angle) * factor
    coarse_ref[1, pl.ds(0, length // FINE)] = jnp.sin(angle) * factor
    rows = lax.broadcasted_iota(jnp.int32, (FINE, width), 0)
    angle = modulo(rows * columns, length).astype(F32) * unit
    coarse_ref[2, pl.ds(0, FINE)] = jnp.cos(angle)
    coarse_ref[3, pl.ds(0, FINE)] = jnp.sin(angle)

    @pl.loop(0, length // FINE)
    def _(block):
        step = 256 if width % 256 == 0 else width
        for left in range(0, width, step):
            cols = pl.ds(left, step)
            cos_c, sin_c = coarse_ref[0, pl.ds(block, 1), cols], coarse_ref[1, pl.ds(block, 1), cols]
            cos_f, sin_f = coarse_ref[2, pl.ds(0, FINE), cols], coarse_ref[3, pl.ds(0, FINE), cols]
            row = pl.ds(pl.multiple_of(block * FINE, FINE), FINE)
            put(row, left, cols, cos_c * cos_f - sin_c * sin_f, sin_c * cos_f + cos_c * sin_f)


def split_rows(own, parts):
    planes, _, ny = own.shape

    def body(own_ref, *refs):
        outs, sems = refs[:-1], refs[-1]
        copies = [
            pltpu.make_async_copy(own_ref.at[:, pl.ds(start, size)], ref, sems.at[i])
            for i, ((start, size), ref) in enumerate(zip(parts, outs))
        ]
        for copy in copies:
            copy.start()
        for copy in copies:
            copy.wait()

    return pl.pallas_call(
        body,
        out_shape=[pltpu.VMEM((planes, size, ny), own.dtype) for _, size in parts],
        in_specs=[pl.BlockSpec(memory_space=pl.ANY)],
        out_specs=[pl.BlockSpec(memory_space=pltpu.VMEM)] * len(parts),
        scratch_shapes=[pltpu.SemaphoreType.DMA((len(parts),))],
        compiler_params=pltpu.CompilerParams(vmem_limit_bytes=8 * MIB),
        cost_estimate=pl.CostEstimate(flops=0, bytes_accessed=MIB, transcendentals=0),
        name="split_rows",
    )(pltpu.with_memory_space_constraint(own, pltpu.HBM))


def prepare(green, contrast, kx_dev, columns_of, slabs):
    ny, nx = green.shape[3], contrast.shape[0]
    args = [green, contrast]

    def body(*refs):
        given, (ty_ref, *tx_refs) = refs[:2], refs[2 : 3 + len(columns_of)]
        count = len(columns_of)
        kept, (coarse_y, *coarse_x, sems) = refs[3 + count : -2 - count], refs[-2 - count :]
        copies = [pltpu.make_async_copy(a, b, sems.at[i]) for i, (a, b) in enumerate(zip(given, kept))]
        for copy in copies:
            copy.start()
        z = lax.axis_index("kslab")
        wide = ny // slabs
        lane = lax.broadcasted_iota(jnp.int32, (1, ny), 1)
        columns = lax.rem(lane // wide + z, slabs) * wide + lane % wide

        def put_y(row, left, cols, cos, sin):
            ty_ref[0, row, cols] = cos.astype(BF16)
            ty_ref[1, row, cols] = sin.astype(BF16)

        fill_table(ny, columns, coarse_y, put_y)
        for blocks, tx_ref, coarse_ref in zip(columns_of, tx_refs, coarse_x):
            total = tx_ref.shape[2]
            lane = lax.broadcasted_iota(jnp.int32, (1, total), 1)
            columns, at = lane, 0
            for m, start, size in blocks:
                here = lax.rem(z + slabs - m, slabs) * kx_dev + start - at + lane
                columns, at = jnp.where(lane >= at, here, columns), at + size

            def put_x(row, left, cols, cos, sin):
                tx_ref[0, row, cols] = cos.astype(BF16)
                tx_ref[1, row, cols] = sin.astype(BF16)

            fill_table(nx, columns, coarse_ref, put_x)
        for copy in copies:
            copy.wait()

    outs = [struct((2, ny, ny), BF16)]
    widths = [-(-sum(size for _, _, size in blocks) // 128) * 128 for blocks in columns_of]
    outs += [struct((2, nx, width), BF16) for width in widths]
    outs += [struct(v.shape, v.dtype) for v in args]
    anywhere, vmem = pl.BlockSpec(memory_space=pl.ANY), pl.BlockSpec(memory_space=pltpu.VMEM)
    made = pl.pallas_call(
        body,
        out_shape=[pltpu.VMEM(o.shape, o.dtype) for o in outs],
        in_specs=[anywhere] * 2,
        out_specs=[vmem] * len(outs),
        scratch_shapes=[
            pltpu.VMEM((4, max(ny // FINE, FINE), ny), F32),
            *[pltpu.VMEM((4, max(nx // FINE, FINE), width), F32) for width in widths],
            pltpu.SemaphoreType.DMA((2,)),
        ],
        compiler_params=pltpu.CompilerParams(vmem_limit_bytes=24 * MIB),
        cost_estimate=pl.CostEstimate(flops=8 * ny * ny, bytes_accessed=8 * MIB, transcendentals=0),
        name="prepare",
    )(*[pltpu.with_memory_space_constraint(v, pltpu.HBM) for v in args])
    return made[0], made[1 : 1 + len(widths)], made[1 + len(widths) :]


def add_sources(total, green_ref, sources, step, start, cols):
    real, imag = total
    whole = pl.ds(pl.multiple_of(start + step * ROWS, ROWS), ROWS)
    for ref, plane, at, layer in sources:
        row = pl.ds(pl.multiple_of(at + step * ROWS, ROWS), ROWS)
        g_real, g_imag = green_ref[layer, 0, whole, cols].astype(F32), green_ref[layer, 1, whole, cols].astype(F32)
        s_real, s_imag = ref[plane, row, cols].astype(F32), ref[plane + 1, row, cols].astype(F32)
        p_real = g_real * s_real - g_imag * s_imag
        p_imag = g_real * s_imag + g_imag * s_real
        real = p_real if real is None else real + p_real
        imag = p_imag if imag is None else imag + p_imag
    return real, imag


def unique(arrays):
    kept = []
    for array in arrays:
        if not any(array is other for other in kept):
            kept.append(array)
    return kept, [next(i for i, other in enumerate(kept) if other is array) for array in arrays]


def early_sum(green, sources, layers, start, size, total=None):
    arrays, at = unique([array for array, _, _ in sources])
    ny = arrays[0].shape[2]

    def body(green_ref, *refs):
        ins, total_ref = refs[:-1], refs[-1]
        given = [(ins[i], plane, row, layer) for i, (_, plane, row), layer in zip(at, sources, layers())]

        @pl.loop(0, size // ROWS)
        def _(step):
            row = pl.ds(pl.multiple_of(step * ROWS, ROWS), ROWS)
            for left in range(0, ny, 256):
                cols = pl.ds(left, 256)
                begun = (None, None) if total is None else (ins[-1][0, row, cols], ins[-1][1, row, cols])
                total_ref[0, row, cols], total_ref[1, row, cols] = add_sources(
                    begun, green_ref, given, step, start, cols
                )

    flops = 8 * len(sources) * size * ny
    ins = [green, *arrays] + ([] if total is None else [total])
    return call(body, [struct((2, size, ny), F32)], ins, flops=flops)[0]


def finish_rows(green, total, sources, layers, table_y, start, size, slabs):
    arrays, at = unique([array for array, _, _ in sources])
    ny = arrays[0].shape[2]
    wide = ny // slabs

    def body(green_ref, total_ref, table_ref, *refs):
        ins, outs, left_ref = refs[: len(arrays)], refs[len(arrays) : -1], refs[-1]
        given = [(ins[i], plane, row, layer) for i, (_, plane, row), layer in zip(at, sources, layers())]

        @pl.loop(0, size // ROWS)
        def _(step):
            row = pl.ds(pl.multiple_of(step * ROWS, ROWS), ROWS)
            low = pl.ds(pl.multiple_of(size + step * ROWS, ROWS), ROWS)
            for left in range(0, ny, 256):
                cols = pl.ds(left, 256)
                begun = total_ref[0, row, cols], total_ref[1, row, cols]
                real, imag = add_sources(begun, green_ref, given, step, start, cols)
                left_ref[row, pl.ds(left, 256)] = real.astype(BF16)
                left_ref[row, pl.ds(ny + left, 256)] = (-imag).astype(BF16)
                left_ref[low, pl.ds(left, 256)] = imag.astype(BF16)
                left_ref[low, pl.ds(ny + left, 256)] = real.astype(BF16)

        for m, out_ref in enumerate(outs):
            cols = pl.ds(m * wide, wide)
            both = jnp.dot(left_ref[:, pl.ds(0, ny)], table_ref[0, :, cols], preferred_element_type=F32)
            both += jnp.dot(left_ref[:, pl.ds(ny, ny)], table_ref[1, :, cols], preferred_element_type=F32)
            out_ref[0] = both[:size].astype(BF16)
            out_ref[1] = both[size:].astype(BF16)

    outs = [struct((2, size, wide), BF16)] * slabs
    flops = 8 * size * ny * ny
    return call(body, outs, [green, total, table_y, *arrays], [pltpu.VMEM((2 * size, 2 * ny), BF16)], flops)


def transform_x(table_x, blocks, total=None, contrast=None):
    wide = blocks[0].shape[2]
    _, nx, half = table_x.shape
    tall = min(nx, TALL)

    def fill(ins, right_ref):
        start = 0
        for ref in ins[: len(blocks)]:
            real, imag, size = ref[0], ref[1], ref.shape[1]
            top, low = pl.ds(start, size), pl.ds(half + start, size)
            right_ref[top, pl.ds(0, wide)] = real
            right_ref[top, pl.ds(wide, wide)] = imag
            right_ref[low, pl.ds(0, wide)] = -imag
            right_ref[low, pl.ds(wide, wide)] = real
            start += size
        if start < half:
            none = jnp.zeros((half - start, 2 * wide), BF16)
            right_ref[pl.ds(start, half - start), :] = none
            right_ref[pl.ds(half + start, half - start), :] = none

    def product(table_ref, right_ref, row):
        part = jnp.dot(table_ref[0, row, :], right_ref[pl.ds(0, half), :], preferred_element_type=F32)
        return part + jnp.dot(table_ref[1, row, :], right_ref[pl.ds(half, half), :], preferred_element_type=F32)

    def body(table_ref, *refs):
        ins, (out_ref, right_ref) = refs[:-2], refs[-2:]
        fill(ins, right_ref)
        for x in range(0, nx, tall):
            row = pl.ds(x, tall)
            part = product(table_ref, right_ref, row)
            out_ref[row, :] = part if total is None else part + ins[-1][row, :]

    def last_body(table_ref, *refs):
        ins, (out_ref, right_ref, kept_ref, sems) = refs[:-4], refs[-4:]
        total_ref, contrast_ref = ins[-2:]
        fill(ins, right_ref)
        copies = []
        for i, x in enumerate(range(0, nx, tall)):
            row = pl.ds(x, tall)
            part = product(table_ref, right_ref, row) + total_ref[row, :]
            scale = contrast_ref[row, :]
            kept_ref[0, row, :] = (part[:, :wide] * scale).astype(BF16)
            kept_ref[1, row, :] = (part[:, wide:] * scale).astype(BF16)
            copies.append(pltpu.make_async_copy(kept_ref.at[:, row], out_ref.at[:, row], sems.at[i]))
            copies[-1].start()
        for copy in copies:
            copy.wait()

    scratch = [pltpu.VMEM((2 * half, 2 * wide), BF16)]
    flops = 8 * nx * half * wide
    if contrast is None:
        ins = [table_x, *blocks] + ([] if total is None else [total])
        return call(body, [struct((nx, 2 * wide), F32)], ins, scratch, flops)[0]
    ins = [table_x, *blocks, total, contrast]
    return pl.pallas_call(
        last_body,
        out_shape=struct((2, nx, wide), BF16),
        in_specs=[pl.BlockSpec(memory_space=pltpu.VMEM)] * len(ins),
        out_specs=pl.BlockSpec(memory_space=pl.ANY),
        scratch_shapes=scratch + [pltpu.VMEM((2, nx, wide), BF16), pltpu.SemaphoreType.DMA((nx // tall,))],
        compiler_params=pltpu.CompilerParams(vmem_limit_bytes=24 * MIB),
        cost_estimate=pl.CostEstimate(flops=flops, bytes_accessed=4 * MIB, transcendentals=0),
        name="transform_x_last",
    )(*[in_vmem(v) for v in ins])


def on_cube_device(slabs, spectra, green, contrast):
    _, _, kx_dev, _ = spectra.shape
    parts = [(0, kx_dev // 2), (kx_dev // 2, kx_dev // 2)]
    own, green, contrast = spectra[0], green[0], contrast[0]

    swap = [(i, i ^ 1) for i in range(8)]
    out = [(i, i ^ 2 if i % 2 == 0 else i ^ 4) for i in range(8)]

    def send(v, route):
        return lax.ppermute(v, "depth", route)

    def layers(masks):
        def at():
            me = lax.axis_index("depth")
            c = lax.rem(me, 2)
            return [jnp.bitwise_xor(me, jnp.where(c == 0, m0, m1)) for m0, m1 in masks]

        return at

    owns = split_rows(own, parts)
    near = [send(v, out) for v in owns]
    own_swap = send(own, swap)
    columns_of = [[(m, start, size) for m in range(slabs)] for start, size in parts]
    table_y, table_x, (green, contrast) = prepare(green, contrast, kx_dev, columns_of, slabs)
    near_swap = [send(v, swap) for v in near]
    far = [send(own_swap[:, s : s + n], out) for s, n in parts]
    across = [send(v, out) for v in near_swap]

    def hop(m, v):
        return lax.ppermute(v, "kslab", [(k, (k + m) % slabs) for k in range(slabs)])

    halves = []
    for i, (start, size) in enumerate(parts):
        far_swap, across_swap = send(far[i], swap), send(across[i], swap)
        sources = [(owns[i], 0, 0), (own_swap, 0, start), (near[i], 0, 0), (near_swap[i], 0, 0), (far[i], 0, 0)]
        total = early_sum(green, sources, layers([(0, 0), (1, 1), (2, 4), (5, 3), (3, 5)]), start, size)
        sources = [(far_swap, 0, 0), (across[i], 0, 0)]
        total = early_sum(green, sources, layers([(4, 2), (7, 7)]), start, size, total)
        halves.append(finish_rows(green, total, [(across_swap, 0, 0)], layers([(6, 6)]), table_y, start, size, slabs))
    field = None
    for i, slab in enumerate(halves):
        blocks = [slab[0]] + [hop(m, slab[m]) for m in range(1, slabs)]
        field = transform_x(table_x[i], blocks, field, contrast if i == len(parts) - 1 else None)
    return field[None]


def solution(mesh):
    in_specs = (
        P("depth", None, "kslab", None),
        P("depth", None, None, "kslab", None),
        P("depth", None, "kslab"),
    )
    out_specs = P("depth", None, None, "kslab")
    depth, slabs = mesh.shape["depth"], mesh.shape["kslab"]

    def on_device(spectra, green, contrast):
        cube = depth == 8 and spectra.shape[0] == 1 and slabs == 4
        if cube and spectra.shape[2] % 128 == 0 and (spectra.shape[3] // slabs) % 128 == 0:
            return on_cube_device(slabs, spectra, green, contrast)
        return on_any_device(spectra, green, contrast)

    return jax.shard_map(on_device, mesh=mesh, in_specs=in_specs, out_specs=out_specs, check_vma=False)
```

```python
import math

import jax
import jax.numpy as jnp
from jax import lax
from jax.experimental import pallas as pl
from jax.experimental.pallas import tpu as pltpu
from jax.sharding import PartitionSpec as P


F32 = jnp.float32
BF16 = jnp.bfloat16
ROWS = 16
FINE = 32
MIB = 1 << 20
TALL = 128
ROUTES = (
    ((0, 1, 2, 3), (1, 2, 3, 0), (2, 3, 0, 1), (3, 0, 1, 2)),
    ((0, 1, 2, 3), (1, 2, 3, 0), (3, 0, 1, 2), (2, 3, 0, 1)),
)


def fourier_tables(length):
    indices = jnp.arange(length, dtype=jnp.int32)
    products = indices[:, None] * indices[None, :] % length
    angles = products.astype(F32) * (2.0 * math.pi / length)
    factor = 1.0 / math.sqrt(length)
    return (jnp.cos(angles) * factor).astype(BF16), (jnp.sin(angles) * factor).astype(BF16)


def on_any_device(spectra, green, contrast):
    lay_dev, _, kx_dev, ny = spectra.shape
    nx = contrast.shape[1]
    coeffs = green.astype(F32)
    sources = lax.all_gather(spectra, "depth", axis=0, tiled=True).astype(F32)[None]
    real_part = jnp.sum(coeffs[:, :, 0] * sources[:, :, 0] - coeffs[:, :, 1] * sources[:, :, 1], axis=1)
    imag_part = jnp.sum(coeffs[:, :, 0] * sources[:, :, 1] + coeffs[:, :, 1] * sources[:, :, 0], axis=1)
    rounded = jnp.stack([real_part, imag_part], axis=1).astype(BF16)
    table_y = jnp.concatenate(fourier_tables(ny), axis=1)
    rows = lay_dev * kx_dev
    from_real = jnp.dot(rounded[:, 0].reshape(rows, ny), table_y, preferred_element_type=F32)
    from_imag = jnp.dot(rounded[:, 1].reshape(rows, ny), table_y, preferred_element_type=F32)
    halfway_real = (from_real[:, :ny] - from_imag[:, ny:]).reshape(lay_dev, kx_dev, ny)
    halfway_imag = (from_real[:, ny:] + from_imag[:, :ny]).reshape(lay_dev, kx_dev, ny)
    halfway = jnp.stack([halfway_real, halfway_imag], axis=1).astype(BF16)
    table_x = jnp.concatenate(fourier_tables(nx), axis=0)
    stacked = jnp.einsum(
        "ak,nckd->ncad",
        table_x,
        lax.all_to_all(halfway, "kslab", split_axis=3, concat_axis=2, tiled=True),
        preferred_element_type=F32,
    )
    real_part = stacked[:, 0, :nx] - stacked[:, 1, nx:]
    imag_part = stacked[:, 0, nx:] + stacked[:, 1, :nx]
    return (jnp.stack([real_part, imag_part], axis=1) * contrast[:, None]).astype(BF16)


def in_vmem(x):
    return pltpu.with_memory_space_constraint(x, pltpu.VMEM)


def call(body, outs, ins, scratch=(), flops=0, vmem=24 * MIB):
    spec = pl.BlockSpec(memory_space=pltpu.VMEM)
    moved = sum(math.prod(v.shape) * v.dtype.itemsize for v in list(outs) + list(ins))
    return pl.pallas_call(
        body,
        out_shape=[pltpu.VMEM(o.shape, o.dtype) for o in outs],
        in_specs=[spec] * len(ins),
        out_specs=[spec] * len(outs),
        scratch_shapes=list(scratch),
        compiler_params=pltpu.CompilerParams(vmem_limit_bytes=vmem),
        cost_estimate=pl.CostEstimate(flops=flops, bytes_accessed=moved, transcendentals=0),
    )(*[in_vmem(v) for v in ins])


def struct(shape, dtype):
    return jax.ShapeDtypeStruct(shape, dtype)


def modulo(v, length):
    return v & (length - 1) if length & (length - 1) == 0 else lax.rem(v, length)


def at_rank(rank, values):
    picked = values[0]
    for k, value in enumerate(values[1:], 1):
        picked = jnp.where(rank == k, value, picked)
    return picked


def fill_table(length, columns, coarse_ref, put):
    width = columns.shape[1]
    unit = 2.0 * math.pi / length
    factor = 1.0 / math.sqrt(length)
    rows = lax.broadcasted_iota(jnp.int32, (length // FINE, width), 0) * FINE
    angle = modulo(rows * columns, length).astype(F32) * unit
    coarse_ref[0, pl.ds(0, length // FINE)] = jnp.cos(angle) * factor
    coarse_ref[1, pl.ds(0, length // FINE)] = jnp.sin(angle) * factor
    rows = lax.broadcasted_iota(jnp.int32, (FINE, width), 0)
    angle = modulo(rows * columns, length).astype(F32) * unit
    coarse_ref[2, pl.ds(0, FINE)] = jnp.cos(angle)
    coarse_ref[3, pl.ds(0, FINE)] = jnp.sin(angle)

    @pl.loop(0, length // FINE)
    def _(block):
        step = 256 if width % 256 == 0 else width
        for left in range(0, width, step):
            cols = pl.ds(left, step)
            cos_c, sin_c = coarse_ref[0, pl.ds(block, 1), cols], coarse_ref[1, pl.ds(block, 1), cols]
            cos_f, sin_f = coarse_ref[2, pl.ds(0, FINE), cols], coarse_ref[3, pl.ds(0, FINE), cols]
            row = pl.ds(pl.multiple_of(block * FINE, FINE), FINE)
            put(row, left, cols, cos_c * cos_f - sin_c * sin_f, sin_c * cos_f + cos_c * sin_f)


def split_rows(own, parts):
    planes, _, ny = own.shape

    def body(own_ref, *refs):
        outs, sems = refs[:-1], refs[-1]
        copies = [
            pltpu.make_async_copy(own_ref.at[:, pl.ds(start, size)], ref, sems.at[i])
            for i, ((start, size), ref) in enumerate(zip(parts, outs))
        ]
        for copy in copies:
            copy.start()
        for copy in copies:
            copy.wait()

    return pl.pallas_call(
        body,
        out_shape=[pltpu.VMEM((planes, size, ny), own.dtype) for _, size in parts],
        in_specs=[pl.BlockSpec(memory_space=pl.ANY)],
        out_specs=[pl.BlockSpec(memory_space=pltpu.VMEM)] * len(parts),
        scratch_shapes=[pltpu.SemaphoreType.DMA((len(parts),))],
        compiler_params=pltpu.CompilerParams(vmem_limit_bytes=8 * MIB),
        cost_estimate=pl.CostEstimate(flops=0, bytes_accessed=MIB, transcendentals=0),
        name="split_rows",
    )(pltpu.with_memory_space_constraint(own, pltpu.HBM))


def prepare(green, contrast, kx_dev, columns_of, slabs):
    ny, nx = green.shape[3], contrast.shape[0]
    args = [green, contrast]

    def body(*refs):
        given, (ty_ref, *tx_refs) = refs[:2], refs[2 : 3 + len(columns_of)]
        count = len(columns_of)
        kept, (coarse_y, *coarse_x, sems) = refs[3 + count : -2 - count], refs[-2 - count :]
        copies = [pltpu.make_async_copy(a, b, sems.at[i]) for i, (a, b) in enumerate(zip(given, kept))]
        for copy in copies:
            copy.start()
        z = lax.axis_index("kslab")
        wide = ny // slabs
        lane = lax.broadcasted_iota(jnp.int32, (1, ny), 1)
        columns = lane
        core = lax.rem(lax.axis_index("depth"), 2)

        def by_core(*values):
            return jnp.where(core == 0, *[at_rank(z, v) for v in values])

        for m, routes in enumerate(zip(*ROUTES)):
            here = by_core(*routes) * wide - m * wide + lane
            columns = jnp.where(lane >= m * wide, here, columns)

        def put_y(row, left, cols, cos, sin):
            ty_ref[0, row, cols] = cos.astype(BF16)
            ty_ref[1, row, cols] = sin.astype(BF16)

        fill_table(ny, columns, coarse_y, put_y)
        for blocks, tx_ref, coarse_ref in zip(columns_of, tx_refs, coarse_x):
            total = tx_ref.shape[2]
            lane = lax.broadcasted_iota(jnp.int32, (1, total), 1)
            columns, at = lane, 0
            for m, start, size in blocks:
                origins = [[routes[m].index(k) for k in range(slabs)] for routes in ROUTES]
                here = by_core(*origins) * kx_dev + start - at + lane
                columns, at = jnp.where(lane >= at, here, columns), at + size

            def put_x(row, left, cols, cos, sin):
                tx_ref[0, row, cols] = cos.astype(BF16)
                tx_ref[1, row, cols] = sin.astype(BF16)

            fill_table(nx, columns, coarse_ref, put_x)
        for copy in copies:
            copy.wait()

    outs = [struct((2, ny, ny), BF16)]
    widths = [-(-sum(size for _, _, size in blocks) // 128) * 128 for blocks in columns_of]
    outs += [struct((2, nx, width), BF16) for width in widths]
    outs += [struct(v.shape, v.dtype) for v in args]
    anywhere, vmem = pl.BlockSpec(memory_space=pl.ANY), pl.BlockSpec(memory_space=pltpu.VMEM)
    made = pl.pallas_call(
        body,
        out_shape=[pltpu.VMEM(o.shape, o.dtype) for o in outs],
        in_specs=[anywhere] * 2,
        out_specs=[vmem] * len(outs),
        scratch_shapes=[
            pltpu.VMEM((4, max(ny // FINE, FINE), ny), F32),
            *[pltpu.VMEM((4, max(nx // FINE, FINE), width), F32) for width in widths],
            pltpu.SemaphoreType.DMA((2,)),
        ],
        compiler_params=pltpu.CompilerParams(vmem_limit_bytes=24 * MIB),
        cost_estimate=pl.CostEstimate(flops=8 * ny * ny, bytes_accessed=8 * MIB, transcendentals=0),
        name="prepare",
    )(*[pltpu.with_memory_space_constraint(v, pltpu.HBM) for v in args])
    return made[0], made[1 : 1 + len(widths)], made[1 + len(widths) :]


def add_sources(total, green_ref, sources, step, start, cols):
    real, imag = total
    whole = pl.ds(pl.multiple_of(start + step * ROWS, ROWS), ROWS)
    for ref, plane, at, layer in sources:
        row = pl.ds(pl.multiple_of(at + step * ROWS, ROWS), ROWS)
        g_real, g_imag = green_ref[layer, 0, whole, cols].astype(F32), green_ref[layer, 1, whole, cols].astype(F32)
        s_real, s_imag = ref[plane, row, cols].astype(F32), ref[plane + 1, row, cols].astype(F32)
        p_real = g_real * s_real - g_imag * s_imag
        p_imag = g_real * s_imag + g_imag * s_real
        real = p_real if real is None else real + p_real
        imag = p_imag if imag is None else imag + p_imag
    return real, imag


def unique(arrays):
    kept = []
    for array in arrays:
        if not any(array is other for other in kept):
            kept.append(array)
    return kept, [next(i for i, other in enumerate(kept) if other is array) for array in arrays]


def early_sum(green, sources, layers, start, size, total=None):
    arrays, at = unique([array for array, _, _ in sources])
    ny = arrays[0].shape[2]

    def body(green_ref, *refs):
        ins, total_ref = refs[:-1], refs[-1]
        given = [(ins[i], plane, row, layer) for i, (_, plane, row), layer in zip(at, sources, layers())]

        @pl.loop(0, size // ROWS)
        def _(step):
            row = pl.ds(pl.multiple_of(step * ROWS, ROWS), ROWS)
            for left in range(0, ny, 256):
                cols = pl.ds(left, 256)
                begun = (None, None) if total is None else (ins[-1][0, row, cols], ins[-1][1, row, cols])
                total_ref[0, row, cols], total_ref[1, row, cols] = add_sources(
                    begun, green_ref, given, step, start, cols
                )

    flops = 8 * len(sources) * size * ny
    ins = [green, *arrays] + ([] if total is None else [total])
    return call(body, [struct((2, size, ny), F32)], ins, flops=flops)[0]


def finish_rows(green, total, sources, layers, table_y, start, size, slabs):
    arrays, at = unique([array for array, _, _ in sources])
    ny = arrays[0].shape[2]
    wide = ny // slabs

    def body(green_ref, total_ref, table_ref, *refs):
        ins, outs, left_ref = refs[: len(arrays)], refs[len(arrays) : -1], refs[-1]
        given = [(ins[i], plane, row, layer) for i, (_, plane, row), layer in zip(at, sources, layers())]

        @pl.loop(0, size // ROWS)
        def _(step):
            row = pl.ds(pl.multiple_of(step * ROWS, ROWS), ROWS)
            low = pl.ds(pl.multiple_of(size + step * ROWS, ROWS), ROWS)
            for left in range(0, ny, 256):
                cols = pl.ds(left, 256)
                begun = total_ref[0, row, cols], total_ref[1, row, cols]
                real, imag = add_sources(begun, green_ref, given, step, start, cols)
                left_ref[row, pl.ds(left, 256)] = real.astype(BF16)
                left_ref[row, pl.ds(ny + left, 256)] = (-imag).astype(BF16)
                left_ref[low, pl.ds(left, 256)] = imag.astype(BF16)
                left_ref[low, pl.ds(ny + left, 256)] = real.astype(BF16)

        for m, out_ref in enumerate(outs):
            cols = pl.ds(m * wide, wide)
            both = jnp.dot(left_ref[:, pl.ds(0, ny)], table_ref[0, :, cols], preferred_element_type=F32)
            both += jnp.dot(left_ref[:, pl.ds(ny, ny)], table_ref[1, :, cols], preferred_element_type=F32)
            out_ref[0] = both[:size].astype(BF16)
            out_ref[1] = both[size:].astype(BF16)

    outs = [struct((2, size, wide), BF16)] * slabs
    flops = 8 * size * ny * ny
    return call(body, outs, [green, total, table_y, *arrays], [pltpu.VMEM((2 * size, 2 * ny), BF16)], flops)


def transform_x(table_x, blocks, total=None, contrast=None):
    wide = blocks[0].shape[2]
    _, nx, half = table_x.shape
    tall = min(nx, TALL)

    def fill(ins, right_ref):
        start = 0
        for ref in ins[: len(blocks)]:
            real, imag, size = ref[0], ref[1], ref.shape[1]
            top, low = pl.ds(start, size), pl.ds(half + start, size)
            right_ref[top, pl.ds(0, wide)] = real
            right_ref[top, pl.ds(wide, wide)] = imag
            right_ref[low, pl.ds(0, wide)] = -imag
            right_ref[low, pl.ds(wide, wide)] = real
            start += size
        if start < half:
            none = jnp.zeros((half - start, 2 * wide), BF16)
            right_ref[pl.ds(start, half - start), :] = none
            right_ref[pl.ds(half + start, half - start), :] = none

    def product(table_ref, right_ref, row):
        part = jnp.dot(table_ref[0, row, :], right_ref[pl.ds(0, half), :], preferred_element_type=F32)
        return part + jnp.dot(table_ref[1, row, :], right_ref[pl.ds(half, half), :], preferred_element_type=F32)

    def body(table_ref, *refs):
        ins, (out_ref, right_ref) = refs[:-2], refs[-2:]
        fill(ins, right_ref)
        for x in range(0, nx, tall):
            row = pl.ds(x, tall)
            part = product(table_ref, right_ref, row)
            out_ref[row, :] = part if total is None else part + ins[-1][row, :]

    def last_body(table_ref, *refs):
        ins, (out_ref, right_ref, kept_ref, sems) = refs[:-4], refs[-4:]
        total_ref, contrast_ref = ins[-2:]
        fill(ins, right_ref)
        copies = []
        for i, x in enumerate(range(0, nx, tall)):
            row = pl.ds(x, tall)
            part = product(table_ref, right_ref, row) + total_ref[row, :]
            scale = contrast_ref[row, :]
            kept_ref[0, row, :] = (part[:, :wide] * scale).astype(BF16)
            kept_ref[1, row, :] = (part[:, wide:] * scale).astype(BF16)
            copies.append(pltpu.make_async_copy(kept_ref.at[:, row], out_ref.at[:, row], sems.at[i]))
            copies[-1].start()
        for copy in copies:
            copy.wait()

    scratch = [pltpu.VMEM((2 * half, 2 * wide), BF16)]
    flops = 8 * nx * half * wide
    if contrast is None:
        ins = [table_x, *blocks] + ([] if total is None else [total])
        return call(body, [struct((nx, 2 * wide), F32)], ins, scratch, flops)[0]
    ins = [table_x, *blocks, total, contrast]
    return pl.pallas_call(
        last_body,
        out_shape=struct((2, nx, wide), BF16),
        in_specs=[pl.BlockSpec(memory_space=pltpu.VMEM)] * len(ins),
        out_specs=pl.BlockSpec(memory_space=pl.ANY),
        scratch_shapes=scratch + [pltpu.VMEM((2, nx, wide), BF16), pltpu.SemaphoreType.DMA((nx // tall,))],
        compiler_params=pltpu.CompilerParams(vmem_limit_bytes=24 * MIB),
        cost_estimate=pl.CostEstimate(flops=flops, bytes_accessed=4 * MIB, transcendentals=0),
        name="transform_x_last",
    )(*[in_vmem(v) for v in ins])


def on_cube_device(slabs, spectra, green, contrast):
    _, _, kx_dev, _ = spectra.shape
    parts = [(0, kx_dev // 2), (kx_dev // 2, kx_dev // 2)]
    own, green, contrast = spectra[0], green[0], contrast[0]

    swap = [(i, i ^ 1) for i in range(8)]
    out = [(i, i ^ 2 if i % 2 == 0 else i ^ 4) for i in range(8)]

    def send(v, route):
        return lax.ppermute(v, "depth", route)

    def layers(masks):
        def at():
            me = lax.axis_index("depth")
            c = lax.rem(me, 2)
            return [jnp.bitwise_xor(me, jnp.where(c == 0, m0, m1)) for m0, m1 in masks]

        return at

    owns = split_rows(own, parts)
    near = [send(v, out) for v in owns]
    own_swap = send(own, swap)
    columns_of = [[(m, start, size) for m in range(slabs)] for start, size in parts]
    table_y, table_x, (green, contrast) = prepare(green, contrast, kx_dev, columns_of, slabs)
    near_swap = [send(v, swap) for v in near]
    far = [send(own_swap[:, s : s + n], out) for s, n in parts]
    across = [send(v, out) for v in near_swap]

    def hop(m, v):
        pairs = [(d * slabs + k, d * slabs + ROUTES[d % 2][m][k]) for d in range(8) for k in range(slabs)]
        return lax.ppermute(v, ("depth", "kslab"), pairs)

    halves = []
    for i, (start, size) in enumerate(parts):
        far_swap, across_swap = send(far[i], swap), send(across[i], swap)
        sources = [(owns[i], 0, 0), (own_swap, 0, start), (near[i], 0, 0), (near_swap[i], 0, 0), (far[i], 0, 0)]
        total = early_sum(green, sources, layers([(0, 0), (1, 1), (2, 4), (5, 3), (3, 5)]), start, size)
        sources = [(far_swap, 0, 0), (across[i], 0, 0)]
        total = early_sum(green, sources, layers([(4, 2), (7, 7)]), start, size, total)
        halves.append(finish_rows(green, total, [(across_swap, 0, 0)], layers([(6, 6)]), table_y, start, size, slabs))
    field = None
    for i, slab in enumerate(halves):
        blocks = [slab[0]] + [hop(m, slab[m]) for m in range(1, slabs)]
        field = transform_x(table_x[i], blocks, field, contrast if i == len(parts) - 1 else None)
    return field[None]


def solution(mesh):
    in_specs = (
        P("depth", None, "kslab", None),
        P("depth", None, None, "kslab", None),
        P("depth", None, "kslab"),
    )
    out_specs = P("depth", None, None, "kslab")
    depth, slabs = mesh.shape["depth"], mesh.shape["kslab"]

    def on_device(spectra, green, contrast):
        cube = depth == 8 and spectra.shape[0] == 1 and slabs == 4
        if cube and spectra.shape[2] % 128 == 0 and (spectra.shape[3] // slabs) % 128 == 0:
            return on_cube_device(slabs, spectra, green, contrast)
        return on_any_device(spectra, green, contrast)

    return jax.shard_map(on_device, mesh=mesh, in_specs=in_specs, out_specs=out_specs, check_vma=False)
```

```python
import math

import jax
import jax.numpy as jnp
from jax import lax
from jax.experimental import pallas as pl
from jax.experimental.pallas import tpu as pltpu
from jax.sharding import PartitionSpec as P


F32 = jnp.float32
BF16 = jnp.bfloat16
ROWS = 16
FINE = 32
MIB = 1 << 20
TALL = 128
ROUTES = (
    ((0, 1, 2, 3), (1, 2, 3, 0), (2, 3, 0, 1), (3, 0, 1, 2)),
    ((0, 1, 2, 3), (1, 2, 3, 0), (3, 0, 1, 2), (2, 3, 0, 1)),
)


def fourier_tables(length):
    indices = jnp.arange(length, dtype=jnp.int32)
    products = indices[:, None] * indices[None, :] % length
    angles = products.astype(F32) * (2.0 * math.pi / length)
    factor = 1.0 / math.sqrt(length)
    return (jnp.cos(angles) * factor).astype(BF16), (jnp.sin(angles) * factor).astype(BF16)


def on_any_device(spectra, green, contrast):
    lay_dev, _, kx_dev, ny = spectra.shape
    nx = contrast.shape[1]
    coeffs = green.astype(F32)
    sources = lax.all_gather(spectra, "depth", axis=0, tiled=True).astype(F32)[None]
    real_part = jnp.sum(coeffs[:, :, 0] * sources[:, :, 0] - coeffs[:, :, 1] * sources[:, :, 1], axis=1)
    imag_part = jnp.sum(coeffs[:, :, 0] * sources[:, :, 1] + coeffs[:, :, 1] * sources[:, :, 0], axis=1)
    rounded = jnp.stack([real_part, imag_part], axis=1).astype(BF16)
    table_y = jnp.concatenate(fourier_tables(ny), axis=1)
    rows = lay_dev * kx_dev
    from_real = jnp.dot(rounded[:, 0].reshape(rows, ny), table_y, preferred_element_type=F32)
    from_imag = jnp.dot(rounded[:, 1].reshape(rows, ny), table_y, preferred_element_type=F32)
    halfway_real = (from_real[:, :ny] - from_imag[:, ny:]).reshape(lay_dev, kx_dev, ny)
    halfway_imag = (from_real[:, ny:] + from_imag[:, :ny]).reshape(lay_dev, kx_dev, ny)
    halfway = jnp.stack([halfway_real, halfway_imag], axis=1).astype(BF16)
    table_x = jnp.concatenate(fourier_tables(nx), axis=0)
    stacked = jnp.einsum(
        "ak,nckd->ncad",
        table_x,
        lax.all_to_all(halfway, "kslab", split_axis=3, concat_axis=2, tiled=True),
        preferred_element_type=F32,
    )
    real_part = stacked[:, 0, :nx] - stacked[:, 1, nx:]
    imag_part = stacked[:, 0, nx:] + stacked[:, 1, :nx]
    return (jnp.stack([real_part, imag_part], axis=1) * contrast[:, None]).astype(BF16)


def in_vmem(x):
    return pltpu.with_memory_space_constraint(x, pltpu.VMEM)


def call(body, outs, ins, scratch=(), flops=0, vmem=24 * MIB):
    spec = pl.BlockSpec(memory_space=pltpu.VMEM)
    moved = sum(math.prod(v.shape) * v.dtype.itemsize for v in list(outs) + list(ins))
    return pl.pallas_call(
        body,
        out_shape=[pltpu.VMEM(o.shape, o.dtype) for o in outs],
        in_specs=[spec] * len(ins),
        out_specs=[spec] * len(outs),
        scratch_shapes=list(scratch),
        compiler_params=pltpu.CompilerParams(vmem_limit_bytes=vmem),
        cost_estimate=pl.CostEstimate(flops=flops, bytes_accessed=moved, transcendentals=0),
    )(*[in_vmem(v) for v in ins])


def struct(shape, dtype):
    return jax.ShapeDtypeStruct(shape, dtype)


def modulo(v, length):
    return v & (length - 1) if length & (length - 1) == 0 else lax.rem(v, length)


def at_rank(rank, values):
    picked = values[0]
    for k, value in enumerate(values[1:], 1):
        picked = jnp.where(rank == k, value, picked)
    return picked


def fill_table(length, columns, coarse_ref, put):
    width = columns.shape[1]
    unit = 2.0 * math.pi / length
    factor = 1.0 / math.sqrt(length)
    rows = lax.broadcasted_iota(jnp.int32, (length // FINE, width), 0) * FINE
    angle = modulo(rows * columns, length).astype(F32) * unit
    coarse_ref[0, pl.ds(0, length // FINE)] = jnp.cos(angle) * factor
    coarse_ref[1, pl.ds(0, length // FINE)] = jnp.sin(angle) * factor
    rows = lax.broadcasted_iota(jnp.int32, (FINE, width), 0)
    angle = modulo(rows * columns, length).astype(F32) * unit
    coarse_ref[2, pl.ds(0, FINE)] = jnp.cos(angle)
    coarse_ref[3, pl.ds(0, FINE)] = jnp.sin(angle)

    @pl.loop(0, length // FINE)
    def _(block):
        step = 256 if width % 256 == 0 else width
        for left in range(0, width, step):
            cols = pl.ds(left, step)
            cos_c, sin_c = coarse_ref[0, pl.ds(block, 1), cols], coarse_ref[1, pl.ds(block, 1), cols]
            cos_f, sin_f = coarse_ref[2, pl.ds(0, FINE), cols], coarse_ref[3, pl.ds(0, FINE), cols]
            row = pl.ds(pl.multiple_of(block * FINE, FINE), FINE)
            put(row, left, cols, cos_c * cos_f - sin_c * sin_f, sin_c * cos_f + cos_c * sin_f)


def split_rows(own, parts):
    planes, _, ny = own.shape

    def body(own_ref, *refs):
        outs, sems = refs[:-1], refs[-1]
        copies = [
            pltpu.make_async_copy(own_ref.at[:, pl.ds(start, size)], ref, sems.at[i])
            for i, ((start, size), ref) in enumerate(zip(parts, outs))
        ]
        for copy in copies:
            copy.start()
        for copy in copies:
            copy.wait()

    return pl.pallas_call(
        body,
        out_shape=[pltpu.VMEM((planes, size, ny), own.dtype) for _, size in parts],
        in_specs=[pl.BlockSpec(memory_space=pl.ANY)],
        out_specs=[pl.BlockSpec(memory_space=pltpu.VMEM)] * len(parts),
        scratch_shapes=[pltpu.SemaphoreType.DMA((len(parts),))],
        compiler_params=pltpu.CompilerParams(vmem_limit_bytes=8 * MIB),
        cost_estimate=pl.CostEstimate(flops=0, bytes_accessed=MIB, transcendentals=0),
        name="split_rows",
    )(pltpu.with_memory_space_constraint(own, pltpu.HBM))


def prepare(green, contrast, kx_dev, columns_of, slabs):
    ny, nx = green.shape[3], contrast.shape[0]
    args = [green, contrast]

    def body(*refs):
        given, (ty_ref, *tx_refs) = refs[:2], refs[2 : 3 + len(columns_of)]
        count = len(columns_of)
        kept, (coarse_y, *coarse_x, sems) = refs[3 + count : -2 - count], refs[-2 - count :]
        copies = [pltpu.make_async_copy(a, b, sems.at[i]) for i, (a, b) in enumerate(zip(given, kept))]
        for copy in copies:
            copy.start()
        z = lax.axis_index("kslab")
        wide = ny // slabs
        lane = lax.broadcasted_iota(jnp.int32, (1, ny), 1)
        columns = lane
        core = lax.rem(lax.axis_index("depth"), 2)

        def by_core(*values):
            return jnp.where(core == 0, *[at_rank(z, v) for v in values])

        for m, routes in enumerate(zip(*ROUTES)):
            here = by_core(*routes) * wide - m * wide + lane
            columns = jnp.where(lane >= m * wide, here, columns)

        def put_y(row, left, cols, cos, sin):
            ty_ref[0, row, cols] = cos.astype(BF16)
            ty_ref[1, row, cols] = sin.astype(BF16)

        fill_table(ny, columns, coarse_y, put_y)
        for blocks, tx_ref, coarse_ref in zip(columns_of, tx_refs, coarse_x):
            total = tx_ref.shape[2]
            lane = lax.broadcasted_iota(jnp.int32, (1, total), 1)
            columns, at = lane, 0
            for m, start, size in blocks:
                origins = [[routes[m].index(k) for k in range(slabs)] for routes in ROUTES]
                here = by_core(*origins) * kx_dev + start - at + lane
                columns, at = jnp.where(lane >= at, here, columns), at + size

            def put_x(row, left, cols, cos, sin):
                tx_ref[0, row, cols] = cos.astype(BF16)
                tx_ref[1, row, cols] = sin.astype(BF16)

            fill_table(nx, columns, coarse_ref, put_x)
        for copy in copies:
            copy.wait()

    outs = [struct((2, ny, ny), BF16)]
    widths = [-(-sum(size for _, _, size in blocks) // 128) * 128 for blocks in columns_of]
    outs += [struct((2, nx, width), BF16) for width in widths]
    outs += [struct(v.shape, v.dtype) for v in args]
    anywhere, vmem = pl.BlockSpec(memory_space=pl.ANY), pl.BlockSpec(memory_space=pltpu.VMEM)
    made = pl.pallas_call(
        body,
        out_shape=[pltpu.VMEM(o.shape, o.dtype) for o in outs],
        in_specs=[anywhere] * 2,
        out_specs=[vmem] * len(outs),
        scratch_shapes=[
            pltpu.VMEM((4, max(ny // FINE, FINE), ny), F32),
            *[pltpu.VMEM((4, max(nx // FINE, FINE), width), F32) for width in widths],
            pltpu.SemaphoreType.DMA((2,)),
        ],
        compiler_params=pltpu.CompilerParams(vmem_limit_bytes=24 * MIB),
        cost_estimate=pl.CostEstimate(flops=8 * ny * ny, bytes_accessed=8 * MIB, transcendentals=0),
        name="prepare",
    )(*[pltpu.with_memory_space_constraint(v, pltpu.HBM) for v in args])
    return made[0], made[1 : 1 + len(widths)], made[1 + len(widths) :]


def add_sources(total, green_ref, sources, step, start, cols):
    real, imag = total
    whole = pl.ds(pl.multiple_of(start + step * ROWS, ROWS), ROWS)
    for ref, plane, at, layer in sources:
        row = pl.ds(pl.multiple_of(at + step * ROWS, ROWS), ROWS)
        g_real, g_imag = green_ref[layer, 0, whole, cols].astype(F32), green_ref[layer, 1, whole, cols].astype(F32)
        s_real, s_imag = ref[plane, row, cols].astype(F32), ref[plane + 1, row, cols].astype(F32)
        p_real = g_real * s_real - g_imag * s_imag
        p_imag = g_real * s_imag + g_imag * s_real
        real = p_real if real is None else real + p_real
        imag = p_imag if imag is None else imag + p_imag
    return real, imag


def unique(arrays):
    kept = []
    for array in arrays:
        if not any(array is other for other in kept):
            kept.append(array)
    return kept, [next(i for i, other in enumerate(kept) if other is array) for array in arrays]


def early_sum(green, sources, layers, start, size, total=None):
    arrays, at = unique([array for array, _, _ in sources])
    ny = arrays[0].shape[2]

    def body(green_ref, *refs):
        ins, total_ref = refs[:-1], refs[-1]
        given = [(ins[i], plane, row, layer) for i, (_, plane, row), layer in zip(at, sources, layers())]

        @pl.loop(0, size // ROWS)
        def _(step):
            row = pl.ds(pl.multiple_of(step * ROWS, ROWS), ROWS)
            for left in range(0, ny, 128):
                cols = pl.ds(left, 128)
                begun = (None, None) if total is None else (ins[-1][0, row, cols], ins[-1][1, row, cols])
                total_ref[0, row, cols], total_ref[1, row, cols] = add_sources(
                    begun, green_ref, given, step, start, cols
                )

    flops = 8 * len(sources) * size * ny
    ins = [green, *arrays] + ([] if total is None else [total])
    return call(body, [struct((2, size, ny), F32)], ins, flops=flops)[0]


def finish_rows(green, total, sources, layers, table_y, start, size, slabs):
    arrays, at = unique([array for array, _, _ in sources])
    ny = arrays[0].shape[2]
    wide = ny // slabs

    def body(green_ref, total_ref, table_ref, *refs):
        ins, outs, left_ref = refs[: len(arrays)], refs[len(arrays) : -1], refs[-1]
        given = [(ins[i], plane, row, layer) for i, (_, plane, row), layer in zip(at, sources, layers())]

        @pl.loop(0, size // ROWS)
        def _(step):
            row = pl.ds(pl.multiple_of(step * ROWS, ROWS), ROWS)
            low = pl.ds(pl.multiple_of(size + step * ROWS, ROWS), ROWS)
            for left in range(0, ny, 128):
                cols = pl.ds(left, 128)
                begun = total_ref[0, row, cols], total_ref[1, row, cols]
                real, imag = add_sources(begun, green_ref, given, step, start, cols)
                left_ref[row, pl.ds(left, 128)] = real.astype(BF16)
                left_ref[row, pl.ds(ny + left, 128)] = (-imag).astype(BF16)
                left_ref[low, pl.ds(left, 128)] = imag.astype(BF16)
                left_ref[low, pl.ds(ny + left, 128)] = real.astype(BF16)

        for m, out_ref in enumerate(outs):
            cols = pl.ds(m * wide, wide)
            both = jnp.dot(left_ref[:, pl.ds(0, ny)], table_ref[0, :, cols], preferred_element_type=F32)
            both += jnp.dot(left_ref[:, pl.ds(ny, ny)], table_ref[1, :, cols], preferred_element_type=F32)
            out_ref[0] = both[:size].astype(BF16)
            out_ref[1] = both[size:].astype(BF16)

    outs = [struct((2, size, wide), BF16)] * slabs
    flops = 8 * size * ny * ny
    return call(body, outs, [green, total, table_y, *arrays], [pltpu.VMEM((2 * size, 2 * ny), BF16)], flops)


def transform_x(table_x, blocks, total=None, contrast=None):
    wide = blocks[0].shape[2]
    _, nx, half = table_x.shape
    tall = min(nx, TALL)

    def fill(ins, right_ref):
        start = 0
        for ref in ins[: len(blocks)]:
            real, imag, size = ref[0], ref[1], ref.shape[1]
            top, low = pl.ds(start, size), pl.ds(half + start, size)
            right_ref[top, pl.ds(0, wide)] = real
            right_ref[top, pl.ds(wide, wide)] = imag
            right_ref[low, pl.ds(0, wide)] = -imag
            right_ref[low, pl.ds(wide, wide)] = real
            start += size
        if start < half:
            none = jnp.zeros((half - start, 2 * wide), BF16)
            right_ref[pl.ds(start, half - start), :] = none
            right_ref[pl.ds(half + start, half - start), :] = none

    def product(table_ref, right_ref, row):
        part = jnp.dot(table_ref[0, row, :], right_ref[pl.ds(0, half), :], preferred_element_type=F32)
        return part + jnp.dot(table_ref[1, row, :], right_ref[pl.ds(half, half), :], preferred_element_type=F32)

    def body(table_ref, *refs):
        ins, (out_ref, right_ref) = refs[:-2], refs[-2:]
        fill(ins, right_ref)
        for x in range(0, nx, tall):
            row = pl.ds(x, tall)
            part = product(table_ref, right_ref, row)
            out_ref[row, :] = part if total is None else part + ins[-1][row, :]

    def last_body(table_ref, *refs):
        ins, (out_ref, right_ref, kept_ref, sems) = refs[:-4], refs[-4:]
        total_ref, contrast_ref = ins[-2:]
        fill(ins, right_ref)
        copies = []
        for i, x in enumerate(range(0, nx, tall)):
            row = pl.ds(x, tall)
            part = product(table_ref, right_ref, row) + total_ref[row, :]
            scale = contrast_ref[row, :]
            kept_ref[0, row, :] = (part[:, :wide] * scale).astype(BF16)
            kept_ref[1, row, :] = (part[:, wide:] * scale).astype(BF16)
            copies.append(pltpu.make_async_copy(kept_ref.at[:, row], out_ref.at[:, row], sems.at[i]))
            copies[-1].start()
        for copy in copies:
            copy.wait()

    scratch = [pltpu.VMEM((2 * half, 2 * wide), BF16)]
    flops = 8 * nx * half * wide
    if contrast is None:
        ins = [table_x, *blocks] + ([] if total is None else [total])
        return call(body, [struct((nx, 2 * wide), F32)], ins, scratch, flops)[0]
    ins = [table_x, *blocks, total, contrast]
    return pl.pallas_call(
        last_body,
        out_shape=struct((2, nx, wide), BF16),
        in_specs=[pl.BlockSpec(memory_space=pltpu.VMEM)] * len(ins),
        out_specs=pl.BlockSpec(memory_space=pl.ANY),
        scratch_shapes=scratch + [pltpu.VMEM((2, nx, wide), BF16), pltpu.SemaphoreType.DMA((nx // tall,))],
        compiler_params=pltpu.CompilerParams(vmem_limit_bytes=24 * MIB),
        cost_estimate=pl.CostEstimate(flops=flops, bytes_accessed=4 * MIB, transcendentals=0),
        name="transform_x_last",
    )(*[in_vmem(v) for v in ins])


def on_cube_device(slabs, spectra, green, contrast):
    _, _, kx_dev, _ = spectra.shape
    parts = [(0, kx_dev // 2), (kx_dev // 2, kx_dev // 2)]
    own, green, contrast = spectra[0], green[0], contrast[0]

    swap = [(i, i ^ 1) for i in range(8)]
    out = [(i, i ^ 2 if i % 2 == 0 else i ^ 4) for i in range(8)]

    def send(v, route):
        return lax.ppermute(v, "depth", route)

    def layers(masks):
        def at():
            me = lax.axis_index("depth")
            c = lax.rem(me, 2)
            return [jnp.bitwise_xor(me, jnp.where(c == 0, m0, m1)) for m0, m1 in masks]

        return at

    owns = split_rows(own, parts)
    near = [send(v, out) for v in owns]
    own_swap = send(own, swap)
    columns_of = [[(m, start, size) for m in range(slabs)] for start, size in parts]
    table_y, table_x, (green, contrast) = prepare(green, contrast, kx_dev, columns_of, slabs)
    near_swap = [send(v, swap) for v in near]
    far = [send(own_swap[:, s : s + n], out) for s, n in parts]
    across = [send(v, out) for v in near_swap]

    def hop(m, v):
        pairs = [(d * slabs + k, d * slabs + ROUTES[d % 2][m][k]) for d in range(8) for k in range(slabs)]
        return lax.ppermute(v, ("depth", "kslab"), pairs)

    halves = []
    for i, (start, size) in enumerate(parts):
        far_swap, across_swap = send(far[i], swap), send(across[i], swap)
        sources = [(owns[i], 0, 0), (own_swap, 0, start), (near[i], 0, 0), (near_swap[i], 0, 0), (far[i], 0, 0)]
        total = early_sum(green, sources, layers([(0, 0), (1, 1), (2, 4), (5, 3), (3, 5)]), start, size)
        sources = [(far_swap, 0, 0), (across[i], 0, 0)]
        total = early_sum(green, sources, layers([(4, 2), (7, 7)]), start, size, total)
        halves.append(finish_rows(green, total, [(across_swap, 0, 0)], layers([(6, 6)]), table_y, start, size, slabs))
    field = None
    for i, slab in enumerate(halves):
        blocks = [slab[0]] + [hop(m, slab[m]) for m in range(1, slabs)]
        field = transform_x(table_x[i], blocks, field, contrast if i == len(parts) - 1 else None)
    return field[None]


def solution(mesh):
    in_specs = (
        P("depth", None, "kslab", None),
        P("depth", None, None, "kslab", None),
        P("depth", None, "kslab"),
    )
    out_specs = P("depth", None, None, "kslab")
    depth, slabs = mesh.shape["depth"], mesh.shape["kslab"]

    def on_device(spectra, green, contrast):
        cube = depth == 8 and spectra.shape[0] == 1 and slabs == 4
        if cube and spectra.shape[2] % 128 == 0 and (spectra.shape[3] // slabs) % 128 == 0:
            return on_cube_device(slabs, spectra, green, contrast)
        return on_any_device(spectra, green, contrast)

    return jax.shard_map(on_device, mesh=mesh, in_specs=in_specs, out_specs=out_specs, check_vma=False)
```

```python
import math

import jax
import jax.numpy as jnp
from jax import lax
from jax.experimental import pallas as pl
from jax.experimental.pallas import tpu as pltpu
from jax.sharding import PartitionSpec as P


F32 = jnp.float32
BF16 = jnp.bfloat16
ROWS = 16
FINE = 32
MIB = 1 << 20
TALL = 128
ROUTES = (
    ((0, 1, 2, 3), (1, 2, 3, 0), (2, 3, 0, 1), (3, 0, 1, 2)),
    ((0, 1, 2, 3), (1, 2, 3, 0), (3, 0, 1, 2), (2, 3, 0, 1)),
)


def fourier_tables(length):
    indices = jnp.arange(length, dtype=jnp.int32)
    products = indices[:, None] * indices[None, :] % length
    angles = products.astype(F32) * (2.0 * math.pi / length)
    factor = 1.0 / math.sqrt(length)
    return (jnp.cos(angles) * factor).astype(BF16), (jnp.sin(angles) * factor).astype(BF16)


def on_any_device(spectra, green, contrast):
    lay_dev, _, kx_dev, ny = spectra.shape
    nx = contrast.shape[1]
    coeffs = green.astype(F32)
    sources = lax.all_gather(spectra, "depth", axis=0, tiled=True).astype(F32)[None]
    real_part = jnp.sum(coeffs[:, :, 0] * sources[:, :, 0] - coeffs[:, :, 1] * sources[:, :, 1], axis=1)
    imag_part = jnp.sum(coeffs[:, :, 0] * sources[:, :, 1] + coeffs[:, :, 1] * sources[:, :, 0], axis=1)
    rounded = jnp.stack([real_part, imag_part], axis=1).astype(BF16)
    table_y = jnp.concatenate(fourier_tables(ny), axis=1)
    rows = lay_dev * kx_dev
    from_real = jnp.dot(rounded[:, 0].reshape(rows, ny), table_y, preferred_element_type=F32)
    from_imag = jnp.dot(rounded[:, 1].reshape(rows, ny), table_y, preferred_element_type=F32)
    halfway_real = (from_real[:, :ny] - from_imag[:, ny:]).reshape(lay_dev, kx_dev, ny)
    halfway_imag = (from_real[:, ny:] + from_imag[:, :ny]).reshape(lay_dev, kx_dev, ny)
    halfway = jnp.stack([halfway_real, halfway_imag], axis=1).astype(BF16)
    table_x = jnp.concatenate(fourier_tables(nx), axis=0)
    stacked = jnp.einsum(
        "ak,nckd->ncad",
        table_x,
        lax.all_to_all(halfway, "kslab", split_axis=3, concat_axis=2, tiled=True),
        preferred_element_type=F32,
    )
    real_part = stacked[:, 0, :nx] - stacked[:, 1, nx:]
    imag_part = stacked[:, 0, nx:] + stacked[:, 1, :nx]
    return (jnp.stack([real_part, imag_part], axis=1) * contrast[:, None]).astype(BF16)


def in_vmem(x):
    return pltpu.with_memory_space_constraint(x, pltpu.VMEM)


def call(body, outs, ins, scratch=(), flops=0, vmem=24 * MIB):
    spec = pl.BlockSpec(memory_space=pltpu.VMEM)
    moved = sum(math.prod(v.shape) * v.dtype.itemsize for v in list(outs) + list(ins))
    return pl.pallas_call(
        body,
        out_shape=[pltpu.VMEM(o.shape, o.dtype) for o in outs],
        in_specs=[spec] * len(ins),
        out_specs=[spec] * len(outs),
        scratch_shapes=list(scratch),
        compiler_params=pltpu.CompilerParams(vmem_limit_bytes=vmem),
        cost_estimate=pl.CostEstimate(flops=flops, bytes_accessed=moved, transcendentals=0),
    )(*[in_vmem(v) for v in ins])


def struct(shape, dtype):
    return jax.ShapeDtypeStruct(shape, dtype)


def modulo(v, length):
    return v & (length - 1) if length & (length - 1) == 0 else lax.rem(v, length)


def at_rank(rank, values):
    picked = values[0]
    for k, value in enumerate(values[1:], 1):
        picked = jnp.where(rank == k, value, picked)
    return picked


def fill_table(length, columns, coarse_ref, put):
    width = columns.shape[1]
    unit = 2.0 * math.pi / length
    factor = 1.0 / math.sqrt(length)
    rows = lax.broadcasted_iota(jnp.int32, (length // FINE, width), 0) * FINE
    angle = modulo(rows * columns, length).astype(F32) * unit
    coarse_ref[0, pl.ds(0, length // FINE)] = jnp.cos(angle) * factor
    coarse_ref[1, pl.ds(0, length // FINE)] = jnp.sin(angle) * factor
    rows = lax.broadcasted_iota(jnp.int32, (FINE, width), 0)
    angle = modulo(rows * columns, length).astype(F32) * unit
    coarse_ref[2, pl.ds(0, FINE)] = jnp.cos(angle)
    coarse_ref[3, pl.ds(0, FINE)] = jnp.sin(angle)

    @pl.loop(0, length // FINE)
    def _(block):
        step = 256 if width % 256 == 0 else width
        for left in range(0, width, step):
            cols = pl.ds(left, step)
            cos_c, sin_c = coarse_ref[0, pl.ds(block, 1), cols], coarse_ref[1, pl.ds(block, 1), cols]
            cos_f, sin_f = coarse_ref[2, pl.ds(0, FINE), cols], coarse_ref[3, pl.ds(0, FINE), cols]
            row = pl.ds(pl.multiple_of(block * FINE, FINE), FINE)
            put(row, left, cols, cos_c * cos_f - sin_c * sin_f, sin_c * cos_f + cos_c * sin_f)


def split_rows(own, parts):
    planes, _, ny = own.shape

    def body(own_ref, *refs):
        outs, sems = refs[:-1], refs[-1]
        copies = [
            pltpu.make_async_copy(own_ref.at[:, pl.ds(start, size)], ref, sems.at[i])
            for i, ((start, size), ref) in enumerate(zip(parts, outs))
        ]
        for copy in copies:
            copy.start()
        for copy in copies:
            copy.wait()

    return pl.pallas_call(
        body,
        out_shape=[pltpu.VMEM((planes, size, ny), own.dtype) for _, size in parts],
        in_specs=[pl.BlockSpec(memory_space=pl.ANY)],
        out_specs=[pl.BlockSpec(memory_space=pltpu.VMEM)] * len(parts),
        scratch_shapes=[pltpu.SemaphoreType.DMA((len(parts),))],
        compiler_params=pltpu.CompilerParams(vmem_limit_bytes=8 * MIB),
        cost_estimate=pl.CostEstimate(flops=0, bytes_accessed=MIB, transcendentals=0),
        name="split_rows",
    )(pltpu.with_memory_space_constraint(own, pltpu.HBM))


def prepare(green, contrast, kx_dev, columns_of, slabs):
    ny, nx = green.shape[3], contrast.shape[0]
    args = [green, contrast]

    def body(*refs):
        given, (ty_ref, *tx_refs) = refs[:2], refs[2 : 3 + len(columns_of)]
        count = len(columns_of)
        kept, (coarse_y, *coarse_x, sems) = refs[3 + count : -2 - count], refs[-2 - count :]
        copies = [pltpu.make_async_copy(a, b, sems.at[i]) for i, (a, b) in enumerate(zip(given, kept))]
        for copy in copies:
            copy.start()
        z = lax.axis_index("kslab")
        wide = ny // slabs
        lane = lax.broadcasted_iota(jnp.int32, (1, ny), 1)
        columns = lane
        core = lax.rem(lax.axis_index("depth"), 2)

        def by_core(*values):
            return jnp.where(core == 0, *[at_rank(z, v) for v in values])

        for m, routes in enumerate(zip(*ROUTES)):
            here = by_core(*routes) * wide - m * wide + lane
            columns = jnp.where(lane >= m * wide, here, columns)

        def put_y(row, left, cols, cos, sin):
            ty_ref[0, row, cols] = cos.astype(BF16)
            ty_ref[1, row, cols] = sin.astype(BF16)

        fill_table(ny, columns, coarse_y, put_y)
        for blocks, tx_ref, coarse_ref in zip(columns_of, tx_refs, coarse_x):
            total = tx_ref.shape[2]
            lane = lax.broadcasted_iota(jnp.int32, (1, total), 1)
            columns, at = lane, 0
            for m, start, size in blocks:
                origins = [[routes[m].index(k) for k in range(slabs)] for routes in ROUTES]
                here = by_core(*origins) * kx_dev + start - at + lane
                columns, at = jnp.where(lane >= at, here, columns), at + size

            def put_x(row, left, cols, cos, sin):
                tx_ref[0, row, cols] = cos.astype(BF16)
                tx_ref[1, row, cols] = sin.astype(BF16)

            fill_table(nx, columns, coarse_ref, put_x)
        for copy in copies:
            copy.wait()

    outs = [struct((2, ny, ny), BF16)]
    widths = [-(-sum(size for _, _, size in blocks) // 128) * 128 for blocks in columns_of]
    outs += [struct((2, nx, width), BF16) for width in widths]
    outs += [struct(v.shape, v.dtype) for v in args]
    anywhere, vmem = pl.BlockSpec(memory_space=pl.ANY), pl.BlockSpec(memory_space=pltpu.VMEM)
    made = pl.pallas_call(
        body,
        out_shape=[pltpu.VMEM(o.shape, o.dtype) for o in outs],
        in_specs=[anywhere] * 2,
        out_specs=[vmem] * len(outs),
        scratch_shapes=[
            pltpu.VMEM((4, max(ny // FINE, FINE), ny), F32),
            *[pltpu.VMEM((4, max(nx // FINE, FINE), width), F32) for width in widths],
            pltpu.SemaphoreType.DMA((2,)),
        ],
        compiler_params=pltpu.CompilerParams(vmem_limit_bytes=24 * MIB),
        cost_estimate=pl.CostEstimate(flops=8 * ny * ny, bytes_accessed=8 * MIB, transcendentals=0),
        name="prepare",
    )(*[pltpu.with_memory_space_constraint(v, pltpu.HBM) for v in args])
    return made[0], made[1 : 1 + len(widths)], made[1 + len(widths) :]


def add_sources(total, green_ref, sources, step, start, cols):
    real, imag = total
    whole = pl.ds(pl.multiple_of(start + step * ROWS, ROWS), ROWS)
    for ref, plane, at, layer in sources:
        row = pl.ds(pl.multiple_of(at + step * ROWS, ROWS), ROWS)
        g_real, g_imag = green_ref[layer, 0, whole, cols].astype(F32), green_ref[layer, 1, whole, cols].astype(F32)
        s_real, s_imag = ref[plane, row, cols].astype(F32), ref[plane + 1, row, cols].astype(F32)
        p_real = g_real * s_real - g_imag * s_imag
        p_imag = g_real * s_imag + g_imag * s_real
        real = p_real if real is None else real + p_real
        imag = p_imag if imag is None else imag + p_imag
    return real, imag


def unique(arrays):
    kept = []
    for array in arrays:
        if not any(array is other for other in kept):
            kept.append(array)
    return kept, [next(i for i, other in enumerate(kept) if other is array) for array in arrays]


def early_sum(green, sources, layers, start, size, total=None):
    arrays, at = unique([array for array, _, _ in sources])
    ny = arrays[0].shape[2]

    def body(green_ref, *refs):
        ins, total_ref = refs[:-1], refs[-1]
        given = [(ins[i], plane, row, layer) for i, (_, plane, row), layer in zip(at, sources, layers())]

        @pl.loop(0, size // ROWS)
        def _(step):
            row = pl.ds(pl.multiple_of(step * ROWS, ROWS), ROWS)
            for left in range(0, ny, 256):
                cols = pl.ds(left, 256)
                begun = (None, None) if total is None else (ins[-1][0, row, cols], ins[-1][1, row, cols])
                total_ref[0, row, cols], total_ref[1, row, cols] = add_sources(
                    begun, green_ref, given, step, start, cols
                )

    flops = 8 * len(sources) * size * ny
    ins = [green, *arrays] + ([] if total is None else [total])
    return call(body, [struct((2, size, ny), F32)], ins, flops=flops)[0]


def finish_rows(green, total, sources, layers, table_y, start, size, slabs):
    arrays, at = unique([array for array, _, _ in sources])
    ny = arrays[0].shape[2]
    wide = ny // slabs

    def body(green_ref, total_ref, table_ref, *refs):
        ins, outs, left_ref = refs[: len(arrays)], refs[len(arrays) : -1], refs[-1]
        given = [(ins[i], plane, row, layer) for i, (_, plane, row), layer in zip(at, sources, layers())]

        @pl.loop(0, size // ROWS)
        def _(step):
            row = pl.ds(pl.multiple_of(step * ROWS, ROWS), ROWS)
            low = pl.ds(pl.multiple_of(size + step * ROWS, ROWS), ROWS)
            for left in range(0, ny, 256):
                cols = pl.ds(left, 256)
                begun = total_ref[0, row, cols], total_ref[1, row, cols]
                real, imag = add_sources(begun, green_ref, given, step, start, cols)
                left_ref[row, pl.ds(left, 256)] = real.astype(BF16)
                left_ref[row, pl.ds(ny + left, 256)] = (-imag).astype(BF16)
                left_ref[low, pl.ds(left, 256)] = imag.astype(BF16)
                left_ref[low, pl.ds(ny + left, 256)] = real.astype(BF16)

        for m, out_ref in enumerate(outs):
            cols = pl.ds(m * wide, wide)
            both = jnp.dot(left_ref[:, pl.ds(0, ny)], table_ref[0, :, cols], preferred_element_type=F32)
            both += jnp.dot(left_ref[:, pl.ds(ny, ny)], table_ref[1, :, cols], preferred_element_type=F32)
            out_ref[0] = both[:size].astype(BF16)
            out_ref[1] = both[size:].astype(BF16)

    outs = [struct((2, size, wide), BF16)] * slabs
    flops = 8 * size * ny * ny
    return call(body, outs, [green, total, table_y, *arrays], [pltpu.VMEM((2 * size, 2 * ny), BF16)], flops)


def transform_x(table_x, blocks, total=None, contrast=None):
    wide = blocks[0].shape[2]
    _, nx, half = table_x.shape
    tall = min(nx, TALL)

    def fill(ins, right_ref):
        start = 0
        for ref in ins[: len(blocks)]:
            real, imag, size = ref[0], ref[1], ref.shape[1]
            top, low = pl.ds(start, size), pl.ds(half + start, size)
            right_ref[top, pl.ds(0, wide)] = real
            right_ref[top, pl.ds(wide, wide)] = imag
            right_ref[low, pl.ds(0, wide)] = -imag
            right_ref[low, pl.ds(wide, wide)] = real
            start += size
        if start < half:
            none = jnp.zeros((half - start, 2 * wide), BF16)
            right_ref[pl.ds(start, half - start), :] = none
            right_ref[pl.ds(half + start, half - start), :] = none

    def product(table_ref, right_ref, row):
        part = jnp.dot(table_ref[0, row, :], right_ref[pl.ds(0, half), :], preferred_element_type=F32)
        return part + jnp.dot(table_ref[1, row, :], right_ref[pl.ds(half, half), :], preferred_element_type=F32)

    def body(table_ref, *refs):
        ins, (out_ref, right_ref) = refs[:-2], refs[-2:]
        fill(ins, right_ref)
        for x in range(0, nx, tall):
            row = pl.ds(x, tall)
            part = product(table_ref, right_ref, row)
            out_ref[row, :] = part if total is None else part + ins[-1][row, :]

    def last_body(table_ref, *refs):
        ins, (out_ref, right_ref, kept_ref, sems) = refs[:-4], refs[-4:]
        total_ref, contrast_ref = ins[-2:]
        fill(ins, right_ref)
        copies = []
        for i, x in enumerate(range(0, nx, tall)):
            row = pl.ds(x, tall)
            part = product(table_ref, right_ref, row) + total_ref[row, :]
            scale = contrast_ref[row, :]
            kept_ref[0, row, :] = (part[:, :wide] * scale).astype(BF16)
            kept_ref[1, row, :] = (part[:, wide:] * scale).astype(BF16)
            for c in range(2):
                copies.append(pltpu.make_async_copy(kept_ref.at[c, row], out_ref.at[c, row], sems.at[2 * i + c]))
                copies[-1].start(priority=c)
        for copy in copies:
            copy.wait()

    scratch = [pltpu.VMEM((2 * half, 2 * wide), BF16)]
    flops = 8 * nx * half * wide
    if contrast is None:
        ins = [table_x, *blocks] + ([] if total is None else [total])
        return call(body, [struct((nx, 2 * wide), F32)], ins, scratch, flops)[0]
    ins = [table_x, *blocks, total, contrast]
    return pl.pallas_call(
        last_body,
        out_shape=struct((2, nx, wide), BF16),
        in_specs=[pl.BlockSpec(memory_space=pltpu.VMEM)] * len(ins),
        out_specs=pl.BlockSpec(memory_space=pl.ANY),
        scratch_shapes=scratch + [pltpu.VMEM((2, nx, wide), BF16), pltpu.SemaphoreType.DMA((2 * nx // tall,))],
        compiler_params=pltpu.CompilerParams(vmem_limit_bytes=24 * MIB),
        cost_estimate=pl.CostEstimate(flops=flops, bytes_accessed=4 * MIB, transcendentals=0),
        name="transform_x_last",
    )(*[in_vmem(v) for v in ins])


def on_cube_device(slabs, spectra, green, contrast):
    _, _, kx_dev, _ = spectra.shape
    parts = [(0, kx_dev // 2), (kx_dev // 2, kx_dev // 2)]
    own, green, contrast = spectra[0], green[0], contrast[0]

    swap = [(i, i ^ 1) for i in range(8)]
    out = [(i, i ^ 2 if i % 2 == 0 else i ^ 4) for i in range(8)]

    def send(v, route):
        return lax.ppermute(v, "depth", route)

    def layers(masks):
        def at():
            me = lax.axis_index("depth")
            c = lax.rem(me, 2)
            return [jnp.bitwise_xor(me, jnp.where(c == 0, m0, m1)) for m0, m1 in masks]

        return at

    owns = split_rows(own, parts)
    near = [send(v, out) for v in owns]
    own_swap = send(own, swap)
    columns_of = [[(m, start, size) for m in range(slabs)] for start, size in parts]
    table_y, table_x, (green, contrast) = prepare(green, contrast, kx_dev, columns_of, slabs)
    near_swap = [send(v, swap) for v in near]
    far = [send(own_swap[:, s : s + n], out) for s, n in parts]
    across = [send(v, out) for v in near_swap]

    def hop(m, v):
        pairs = [(d * slabs + k, d * slabs + ROUTES[d % 2][m][k]) for d in range(8) for k in range(slabs)]
        return lax.ppermute(v, ("depth", "kslab"), pairs)

    halves = []
    for i, (start, size) in enumerate(parts):
        far_swap, across_swap = send(far[i], swap), send(across[i], swap)
        sources = [(owns[i], 0, 0), (own_swap, 0, start), (near[i], 0, 0), (near_swap[i], 0, 0), (far[i], 0, 0)]
        total = early_sum(green, sources, layers([(0, 0), (1, 1), (2, 4), (5, 3), (3, 5)]), start, size)
        sources = [(far_swap, 0, 0), (across[i], 0, 0)]
        total = early_sum(green, sources, layers([(4, 2), (7, 7)]), start, size, total)
        halves.append(finish_rows(green, total, [(across_swap, 0, 0)], layers([(6, 6)]), table_y, start, size, slabs))
    field = None
    for i, slab in enumerate(halves):
        blocks = [slab[0]] + [hop(m, slab[m]) for m in range(1, slabs)]
        field = transform_x(table_x[i], blocks, field, contrast if i == len(parts) - 1 else None)
    return field[None]


def solution(mesh):
    in_specs = (
        P("depth", None, "kslab", None),
        P("depth", None, None, "kslab", None),
        P("depth", None, "kslab"),
    )
    out_specs = P("depth", None, None, "kslab")
    depth, slabs = mesh.shape["depth"], mesh.shape["kslab"]

    def on_device(spectra, green, contrast):
        cube = depth == 8 and spectra.shape[0] == 1 and slabs == 4
        if cube and spectra.shape[2] % 128 == 0 and (spectra.shape[3] // slabs) % 128 == 0:
            return on_cube_device(slabs, spectra, green, contrast)
        return on_any_device(spectra, green, contrast)

    return jax.shard_map(on_device, mesh=mesh, in_specs=in_specs, out_specs=out_specs, check_vma=False)
```

```python
import math

import jax
import jax.numpy as jnp
from jax import lax
from jax.experimental import pallas as pl
from jax.experimental.pallas import tpu as pltpu
from jax.sharding import PartitionSpec as P


F32 = jnp.float32
BF16 = jnp.bfloat16
ROWS = 16
FINE = 32
MIB = 1 << 20
TALL = 128
ROUTES = (
    ((0, 1, 2, 3), (1, 2, 3, 0), (2, 3, 0, 1), (3, 0, 1, 2)),
    ((0, 1, 2, 3), (1, 2, 3, 0), (3, 0, 1, 2), (2, 3, 0, 1)),
)


def fourier_tables(length):
    indices = jnp.arange(length, dtype=jnp.int32)
    products = indices[:, None] * indices[None, :] % length
    angles = products.astype(F32) * (2.0 * math.pi / length)
    factor = 1.0 / math.sqrt(length)
    return (jnp.cos(angles) * factor).astype(BF16), (jnp.sin(angles) * factor).astype(BF16)


def on_any_device(spectra, green, contrast):
    lay_dev, _, kx_dev, ny = spectra.shape
    nx = contrast.shape[1]
    coeffs = green.astype(F32)
    sources = lax.all_gather(spectra, "depth", axis=0, tiled=True).astype(F32)[None]
    real_part = jnp.sum(coeffs[:, :, 0] * sources[:, :, 0] - coeffs[:, :, 1] * sources[:, :, 1], axis=1)
    imag_part = jnp.sum(coeffs[:, :, 0] * sources[:, :, 1] + coeffs[:, :, 1] * sources[:, :, 0], axis=1)
    rounded = jnp.stack([real_part, imag_part], axis=1).astype(BF16)
    table_y = jnp.concatenate(fourier_tables(ny), axis=1)
    rows = lay_dev * kx_dev
    from_real = jnp.dot(rounded[:, 0].reshape(rows, ny), table_y, preferred_element_type=F32)
    from_imag = jnp.dot(rounded[:, 1].reshape(rows, ny), table_y, preferred_element_type=F32)
    halfway_real = (from_real[:, :ny] - from_imag[:, ny:]).reshape(lay_dev, kx_dev, ny)
    halfway_imag = (from_real[:, ny:] + from_imag[:, :ny]).reshape(lay_dev, kx_dev, ny)
    halfway = jnp.stack([halfway_real, halfway_imag], axis=1).astype(BF16)
    table_x = jnp.concatenate(fourier_tables(nx), axis=0)
    stacked = jnp.einsum(
        "ak,nckd->ncad",
        table_x,
        lax.all_to_all(halfway, "kslab", split_axis=3, concat_axis=2, tiled=True),
        preferred_element_type=F32,
    )
    real_part = stacked[:, 0, :nx] - stacked[:, 1, nx:]
    imag_part = stacked[:, 0, nx:] + stacked[:, 1, :nx]
    return (jnp.stack([real_part, imag_part], axis=1) * contrast[:, None]).astype(BF16)


def in_vmem(x):
    return pltpu.with_memory_space_constraint(x, pltpu.VMEM)


def call(body, outs, ins, scratch=(), flops=0, vmem=24 * MIB):
    spec = pl.BlockSpec(memory_space=pltpu.VMEM)
    moved = sum(math.prod(v.shape) * v.dtype.itemsize for v in list(outs) + list(ins))
    return pl.pallas_call(
        body,
        out_shape=[pltpu.VMEM(o.shape, o.dtype) for o in outs],
        in_specs=[spec] * len(ins),
        out_specs=[spec] * len(outs),
        scratch_shapes=list(scratch),
        compiler_params=pltpu.CompilerParams(vmem_limit_bytes=vmem),
        cost_estimate=pl.CostEstimate(flops=flops, bytes_accessed=moved, transcendentals=0),
    )(*[in_vmem(v) for v in ins])


def struct(shape, dtype):
    return jax.ShapeDtypeStruct(shape, dtype)


def modulo(v, length):
    return v & (length - 1) if length & (length - 1) == 0 else lax.rem(v, length)


def at_rank(rank, values):
    picked = values[0]
    for k, value in enumerate(values[1:], 1):
        picked = jnp.where(rank == k, value, picked)
    return picked


def fill_table(length, columns, coarse_ref, put):
    width = columns.shape[1]
    unit = 2.0 * math.pi / length
    factor = 1.0 / math.sqrt(length)
    rows = lax.broadcasted_iota(jnp.int32, (length // FINE, width), 0) * FINE
    angle = modulo(rows * columns, length).astype(F32) * unit
    coarse_ref[0, pl.ds(0, length // FINE)] = jnp.cos(angle) * factor
    coarse_ref[1, pl.ds(0, length // FINE)] = jnp.sin(angle) * factor
    rows = lax.broadcasted_iota(jnp.int32, (FINE, width), 0)
    angle = modulo(rows * columns, length).astype(F32) * unit
    coarse_ref[2, pl.ds(0, FINE)] = jnp.cos(angle)
    coarse_ref[3, pl.ds(0, FINE)] = jnp.sin(angle)

    @pl.loop(0, length // FINE)
    def _(block):
        step = 256 if width % 256 == 0 else width
        for left in range(0, width, step):
            cols = pl.ds(left, step)
            cos_c, sin_c = coarse_ref[0, pl.ds(block, 1), cols], coarse_ref[1, pl.ds(block, 1), cols]
            cos_f, sin_f = coarse_ref[2, pl.ds(0, FINE), cols], coarse_ref[3, pl.ds(0, FINE), cols]
            row = pl.ds(pl.multiple_of(block * FINE, FINE), FINE)
            put(row, left, cols, cos_c * cos_f - sin_c * sin_f, sin_c * cos_f + cos_c * sin_f)


def split_rows(own, parts):
    planes, _, ny = own.shape

    def body(own_ref, *refs):
        outs, sems = refs[:-1], refs[-1]
        copies = [
            pltpu.make_async_copy(own_ref.at[:, pl.ds(start, size)], ref, sems.at[i])
            for i, ((start, size), ref) in enumerate(zip(parts, outs))
        ]
        for copy in copies:
            copy.start()
        for copy in copies:
            copy.wait()

    return pl.pallas_call(
        body,
        out_shape=[pltpu.VMEM((planes, size, ny), own.dtype) for _, size in parts],
        in_specs=[pl.BlockSpec(memory_space=pl.ANY)],
        out_specs=[pl.BlockSpec(memory_space=pltpu.VMEM)] * len(parts),
        scratch_shapes=[pltpu.SemaphoreType.DMA((len(parts),))],
        compiler_params=pltpu.CompilerParams(vmem_limit_bytes=8 * MIB),
        cost_estimate=pl.CostEstimate(flops=0, bytes_accessed=MIB, transcendentals=0),
        name="split_rows",
    )(pltpu.with_memory_space_constraint(own, pltpu.HBM))


def prepare(green, contrast, kx_dev, columns_of, slabs):
    ny, nx = green.shape[3], contrast.shape[0]
    args = [green, contrast]

    def body(*refs):
        given, (ty_ref, *tx_refs) = refs[:2], refs[2 : 3 + len(columns_of)]
        count = len(columns_of)
        kept, (coarse_y, *coarse_x, sems) = refs[3 + count : -2 - count], refs[-2 - count :]
        copies = [pltpu.make_async_copy(a, b, sems.at[i]) for i, (a, b) in enumerate(zip(given, kept))]
        for copy in copies:
            copy.start()
        z = lax.axis_index("kslab")
        wide = ny // slabs
        lane = lax.broadcasted_iota(jnp.int32, (1, ny), 1)
        columns = lane
        core = lax.rem(lax.axis_index("depth"), 2)

        def by_core(*values):
            return jnp.where(core == 0, *[at_rank(z, v) for v in values])

        for m, routes in enumerate(zip(*ROUTES)):
            here = by_core(*routes) * wide - m * wide + lane
            columns = jnp.where(lane >= m * wide, here, columns)

        def put_y(row, left, cols, cos, sin):
            ty_ref[0, row, cols] = cos.astype(BF16)
            ty_ref[1, row, cols] = sin.astype(BF16)

        fill_table(ny, columns, coarse_y, put_y)
        for blocks, tx_ref, coarse_ref in zip(columns_of, tx_refs, coarse_x):
            total = tx_ref.shape[2]
            lane = lax.broadcasted_iota(jnp.int32, (1, total), 1)
            columns, at = lane, 0
            for m, start, size in blocks:
                origins = [[routes[m].index(k) for k in range(slabs)] for routes in ROUTES]
                here = by_core(*origins) * kx_dev + start - at + lane
                columns, at = jnp.where(lane >= at, here, columns), at + size

            def put_x(row, left, cols, cos, sin):
                tx_ref[0, row, cols] = cos.astype(BF16)
                tx_ref[1, row, cols] = sin.astype(BF16)

            fill_table(nx, columns, coarse_ref, put_x)
        for copy in copies:
            copy.wait()

    outs = [struct((2, ny, ny), BF16)]
    widths = [-(-sum(size for _, _, size in blocks) // 128) * 128 for blocks in columns_of]
    outs += [struct((2, nx, width), BF16) for width in widths]
    outs += [struct(v.shape, v.dtype) for v in args]
    anywhere, vmem = pl.BlockSpec(memory_space=pl.ANY), pl.BlockSpec(memory_space=pltpu.VMEM)
    made = pl.pallas_call(
        body,
        out_shape=[pltpu.VMEM(o.shape, o.dtype) for o in outs],
        in_specs=[anywhere] * 2,
        out_specs=[vmem] * len(outs),
        scratch_shapes=[
            pltpu.VMEM((4, max(ny // FINE, FINE), ny), F32),
            *[pltpu.VMEM((4, max(nx // FINE, FINE), width), F32) for width in widths],
            pltpu.SemaphoreType.DMA((2,)),
        ],
        compiler_params=pltpu.CompilerParams(vmem_limit_bytes=24 * MIB),
        cost_estimate=pl.CostEstimate(flops=8 * ny * ny, bytes_accessed=8 * MIB, transcendentals=0),
        name="prepare",
    )(*[pltpu.with_memory_space_constraint(v, pltpu.HBM) for v in args])
    return made[0], made[1 : 1 + len(widths)], made[1 + len(widths) :]


def add_sources(total, green_ref, sources, step, start, cols):
    real, imag = total
    whole = pl.ds(pl.multiple_of(start + step * ROWS, ROWS), ROWS)
    for ref, plane, at, layer in sources:
        row = pl.ds(pl.multiple_of(at + step * ROWS, ROWS), ROWS)
        g_real, g_imag = green_ref[layer, 0, whole, cols].astype(F32), green_ref[layer, 1, whole, cols].astype(F32)
        s_real, s_imag = ref[plane, row, cols].astype(F32), ref[plane + 1, row, cols].astype(F32)
        p_real = g_real * s_real - g_imag * s_imag
        p_imag = g_real * s_imag + g_imag * s_real
        real = p_real if real is None else real + p_real
        imag = p_imag if imag is None else imag + p_imag
    return real, imag


def unique(arrays):
    kept = []
    for array in arrays:
        if not any(array is other for other in kept):
            kept.append(array)
    return kept, [next(i for i, other in enumerate(kept) if other is array) for array in arrays]


def early_sum(green, sources, layers, start, size, total=None):
    arrays, at = unique([array for array, _, _ in sources])
    ny = arrays[0].shape[2]

    def body(green_ref, *refs):
        ins, total_ref = refs[:-1], refs[-1]
        given = [(ins[i], plane, row, layer) for i, (_, plane, row), layer in zip(at, sources, layers())]

        @pl.loop(0, size // ROWS)
        def _(step):
            row = pl.ds(pl.multiple_of(step * ROWS, ROWS), ROWS)
            for left in range(0, ny, 256):
                cols = pl.ds(left, 256)
                begun = (None, None) if total is None else (ins[-1][0, row, cols], ins[-1][1, row, cols])
                total_ref[0, row, cols], total_ref[1, row, cols] = add_sources(
                    begun, green_ref, given, step, start, cols
                )

    flops = 8 * len(sources) * size * ny
    ins = [green, *arrays] + ([] if total is None else [total])
    return call(body, [struct((2, size, ny), F32)], ins, flops=flops)[0]


def finish_rows(green, total, sources, layers, table_y, start, size, slabs):
    arrays, at = unique([array for array, _, _ in sources])
    ny = arrays[0].shape[2]
    wide = ny // slabs

    def body(green_ref, total_ref, table_ref, *refs):
        ins, outs, left_ref = refs[: len(arrays)], refs[len(arrays) : -1], refs[-1]
        given = [(ins[i], plane, row, layer) for i, (_, plane, row), layer in zip(at, sources, layers())]

        @pl.loop(0, size // ROWS)
        def _(step):
            row = pl.ds(pl.multiple_of(step * ROWS, ROWS), ROWS)
            low = pl.ds(pl.multiple_of(size + step * ROWS, ROWS), ROWS)
            for left in range(0, ny, 256):
                cols = pl.ds(left, 256)
                begun = total_ref[0, row, cols], total_ref[1, row, cols]
                real, imag = add_sources(begun, green_ref, given, step, start, cols)
                left_ref[row, pl.ds(left, 256)] = real.astype(BF16)
                left_ref[row, pl.ds(ny + left, 256)] = (-imag).astype(BF16)
                left_ref[low, pl.ds(left, 256)] = imag.astype(BF16)
                left_ref[low, pl.ds(ny + left, 256)] = real.astype(BF16)

        for m, out_ref in enumerate(outs):
            cols = pl.ds(m * wide, wide)
            both = jnp.dot(left_ref[:, pl.ds(0, ny)], table_ref[0, :, cols], preferred_element_type=F32)
            both += jnp.dot(left_ref[:, pl.ds(ny, ny)], table_ref[1, :, cols], preferred_element_type=F32)
            out_ref[0] = both[:size].astype(BF16)
            out_ref[1] = both[size:].astype(BF16)

    outs = [struct((2, size, wide), BF16)] * slabs
    flops = 8 * size * ny * ny
    return call(body, outs, [green, total, table_y, *arrays], [pltpu.VMEM((2 * size, 2 * ny), BF16)], flops)


def transform_x(table_x, blocks, total=None, contrast=None):
    wide = blocks[0].shape[2]
    _, nx, half = table_x.shape
    tall = min(nx, TALL)

    def fill(ins, right_ref):
        start = 0
        for ref in ins[: len(blocks)]:
            real, imag, size = ref[0], ref[1], ref.shape[1]
            top, low = pl.ds(start, size), pl.ds(half + start, size)
            right_ref[top, pl.ds(0, wide)] = real
            right_ref[top, pl.ds(wide, wide)] = imag
            right_ref[low, pl.ds(0, wide)] = -imag
            right_ref[low, pl.ds(wide, wide)] = real
            start += size
        if start < half:
            none = jnp.zeros((half - start, 2 * wide), BF16)
            right_ref[pl.ds(start, half - start), :] = none
            right_ref[pl.ds(half + start, half - start), :] = none

    def product(table_ref, right_ref, row):
        part = jnp.dot(table_ref[0, row, :], right_ref[pl.ds(0, half), :], preferred_element_type=F32)
        return part + jnp.dot(table_ref[1, row, :], right_ref[pl.ds(half, half), :], preferred_element_type=F32)

    def body(table_ref, *refs):
        ins, (out_ref, right_ref) = refs[:-2], refs[-2:]
        fill(ins, right_ref)
        for x in range(0, nx, tall):
            row = pl.ds(x, tall)
            part = product(table_ref, right_ref, row)
            out_ref[row, :] = part if total is None else part + ins[-1][row, :]

    def last_body(table_ref, *refs):
        ins, (out_ref, right_ref, kept_ref, sems) = refs[:-4], refs[-4:]
        total_ref, contrast_ref = ins[-2:]
        fill(ins, right_ref)
        copies = []
        for i, x in enumerate(range(0, nx, tall)):
            row = pl.ds(x, tall)
            part = product(table_ref, right_ref, row) + total_ref[row, :]
            scale = contrast_ref[row, :]
            kept_ref[0, row, :] = (part[:, :wide] * scale).astype(BF16)
            kept_ref[1, row, :] = (part[:, wide:] * scale).astype(BF16)
            copies.append(pltpu.make_async_copy(kept_ref.at[:, row], out_ref.at[:, row], sems.at[i]))
            copies[-1].start()
        for copy in copies:
            copy.wait()

    scratch = [pltpu.VMEM((2 * half, 2 * wide), BF16)]
    flops = 8 * nx * half * wide
    if contrast is None:
        ins = [table_x, *blocks] + ([] if total is None else [total])
        return call(body, [struct((nx, 2 * wide), F32)], ins, scratch, flops)[0]
    ins = [table_x, *blocks, total, contrast]
    return pl.pallas_call(
        last_body,
        out_shape=struct((2, nx, wide), BF16),
        in_specs=[pl.BlockSpec(memory_space=pltpu.VMEM)] * len(ins),
        out_specs=pl.BlockSpec(memory_space=pl.ANY),
        scratch_shapes=scratch + [pltpu.VMEM((2, nx, wide), BF16), pltpu.SemaphoreType.DMA((nx // tall,))],
        compiler_params=pltpu.CompilerParams(vmem_limit_bytes=24 * MIB),
        cost_estimate=pl.CostEstimate(flops=flops, bytes_accessed=4 * MIB, transcendentals=0),
        name="transform_x_last",
    )(*[in_vmem(v) for v in ins])


def on_cube_device(slabs, spectra, green, contrast):
    _, _, kx_dev, _ = spectra.shape
    parts = [(0, kx_dev // 2), (kx_dev // 2, kx_dev // 2)]
    own, green, contrast = spectra[0], green[0], contrast[0]

    swap = [(i, i ^ 1) for i in range(8)]
    out = [(i, i ^ 4 if i % 2 == 0 else i ^ 2) for i in range(8)]

    def send(v, route):
        return lax.ppermute(v, "depth", route)

    def layers(masks):
        def at():
            me = lax.axis_index("depth")
            c = lax.rem(me, 2)
            return [jnp.bitwise_xor(me, jnp.where(c == 0, m0, m1)) for m0, m1 in masks]

        return at

    owns = split_rows(own, parts)
    near = [send(v, out) for v in owns]
    own_swap = send(own, swap)
    columns_of = [[(m, start, size) for m in range(slabs)] for start, size in parts]
    table_y, table_x, (green, contrast) = prepare(green, contrast, kx_dev, columns_of, slabs)
    near_swap = [send(v, swap) for v in near]
    far = [send(own_swap[:, s : s + n], out) for s, n in parts]
    across = [send(v, out) for v in near_swap]

    def hop(m, v):
        pairs = [(d * slabs + k, d * slabs + ROUTES[d % 2][m][k]) for d in range(8) for k in range(slabs)]
        return lax.ppermute(v, ("depth", "kslab"), pairs)

    halves = []
    for i, (start, size) in enumerate(parts):
        far_swap, across_swap = send(far[i], swap), send(across[i], swap)
        sources = [(owns[i], 0, 0), (own_swap, 0, start), (near[i], 0, 0), (near_swap[i], 0, 0), (far[i], 0, 0)]
        total = early_sum(green, sources, layers([(0, 0), (1, 1), (4, 2), (3, 5), (5, 3)]), start, size)
        sources = [(far_swap, 0, 0), (across[i], 0, 0)]
        total = early_sum(green, sources, layers([(2, 4), (7, 7)]), start, size, total)
        halves.append(finish_rows(green, total, [(across_swap, 0, 0)], layers([(6, 6)]), table_y, start, size, slabs))
    field = None
    for i, slab in enumerate(halves):
        blocks = [slab[0]] + [hop(m, slab[m]) for m in range(1, slabs)]
        field = transform_x(table_x[i], blocks, field, contrast if i == len(parts) - 1 else None)
    return field[None]


def solution(mesh):
    in_specs = (
        P("depth", None, "kslab", None),
        P("depth", None, None, "kslab", None),
        P("depth", None, "kslab"),
    )
    out_specs = P("depth", None, None, "kslab")
    depth, slabs = mesh.shape["depth"], mesh.shape["kslab"]

    def on_device(spectra, green, contrast):
        cube = depth == 8 and spectra.shape[0] == 1 and slabs == 4
        if cube and spectra.shape[2] % 128 == 0 and (spectra.shape[3] // slabs) % 128 == 0:
            return on_cube_device(slabs, spectra, green, contrast)
        return on_any_device(spectra, green, contrast)

    return jax.shard_map(on_device, mesh=mesh, in_specs=in_specs, out_specs=out_specs, check_vma=False)
```
